256 devices in a mesh: ctx: 64 (over z, x, core), dp: 4 (over y).
Axes of the slice: x: 4, y: 4, z: 8, core: 2. Of those that a mesh axis runs over, the one named last changes fastest.
Arguments:
- query: bfloat16 [4, 32768, 1024], P('dp', 'ctx'), may hold values from -6 to 6
- key: bfloat16 [4, 32768, 1024], P('dp', 'ctx'), may hold values from -6 to 6
- value: bfloat16 [4, 32768, 1024], P('dp', 'ctx'), may hold values from -12 to 12
- log_decay: float32 [4, 8, 32768], P('dp', None, 'ctx'), may hold values from -2 to 0
- grad_out: bfloat16 [4, 32768, 1024], P('dp', 'ctx'), may hold values from -32 to 32
- query_map: bfloat16 [8, 128, 128], replicated, may hold values from -0.5 to 0.5
- key_map: bfloat16 [8, 128, 128], replicated, may hold values from -0.5 to 0.5
Outputs:
- output: bfloat16 [4, 32768, 1024], P('dp', 'ctx')
- grad_query: bfloat16 [4, 32768, 1024], P('dp', 'ctx')
- grad_key: bfloat16 [4, 32768, 1024], P('dp', 'ctx')
- grad_value: bfloat16 [4, 32768, 1024], P('dp', 'ctx')
- query_map_grad: float32 [8, 128, 128], replicated
- key_map_grad: float32 [8, 128, 128], replicated
The draws below stay inside these ranges and needn't reach their ends.
All inputs are finite; a program needn't handle non-finite values.
Results may differ from the reference program's by a relative error of at most 0.0073.
Values sent between devices are 32-bit elements; how exact they have to be, the bound alone decides.
No kernel may reach another device: no remote copies, remote signals or barrier semaphores. Data moves between devices by JAX's collectives and lax.ppermute only.
A program may use at most 128 MiB of HBM per device.

```python
import math
import jax
import jax.numpy as jnp
from jax import lax

LOCAL_HEADS = 8
DH = 128
BLOCK = 256
TOK_DEV = 512
SEQUENCE_LENGTH = 32768
BATCH_SEQUENCES = 4


def decay_plan(key):
    plan_keys = jax.random.split(jax.random.fold_in(key, 7001), 4)
    array_shape = (BATCH_SEQUENCES, LOCAL_HEADS, 1)
    kind_draw = jax.random.randint(plan_keys[0], array_shape, 0, 20)
    fast_limit = 5
    medium_limit = 10
    is_fast = kind_draw < fast_limit
    is_medium = jnp.logical_and(kind_draw >= fast_limit, kind_draw < medium_limit)
    fast_rate = jnp.exp(jax.random.uniform(plan_keys[1], array_shape, jnp.float32, math.log(7.75), math.log(8.53))) / BLOCK
    medium_rate = -jax.random.uniform(plan_keys[2], array_shape, jnp.float32, math.log(0.035), math.log(0.045)) / TOK_DEV
    slow_rate = jnp.exp(jax.random.uniform(plan_keys[3], array_shape, jnp.float32, math.log(0.4), math.log(1.0))) / SEQUENCE_LENGTH
    decay_rate = jnp.where(is_fast, fast_rate, jnp.where(is_medium, medium_rate, slow_rate))
    rate_spread = jnp.where(is_medium, 0.12, 0.35)
    memory_span = jnp.minimum(0.5 / decay_rate, 0.5 * SEQUENCE_LENGTH)
    head_scale = jnp.minimum(3.0, 12.0 / jnp.sqrt(memory_span))
    return (decay_rate, rate_spread, head_scale, is_medium)


def shard_factors(key):
    phase_draw = jax.random.randint(jax.random.fold_in(key, 7002), (BATCH_SEQUENCES, 1), 0, 3)
    shard_kind = (jnp.arange(SEQUENCE_LENGTH)[None, :] // TOK_DEV + phase_draw) % 3
    value_factor = jnp.where(shard_kind == 0, 1.0, 0.125)
    grad_factor = jnp.where(shard_kind == 0, 1.0, jnp.where(shard_kind == 1, 0.125, 8.0))
    return (value_factor, grad_factor)


def column_spread(per_head):
    spread_out = jnp.broadcast_to(per_head, (BATCH_SEQUENCES, LOCAL_HEADS, DH))
    return spread_out.reshape(BATCH_SEQUENCES, 1, LOCAL_HEADS * DH)


def unit_noise(noise_key, array_shape):
    return jnp.clip(jax.random.normal(noise_key, array_shape, jnp.float32), -4.0, 4.0)


def draw_value(key, part):
    _, _, head_scale, is_medium = decay_plan(key)
    value_factor, _ = shard_factors(key)
    noise = unit_noise(jax.random.fold_in(key, 7004), (BATCH_SEQUENCES, SEQUENCE_LENGTH, LOCAL_HEADS * DH))
    medium_cols = column_spread(is_medium.astype(jnp.float32))
    shard_scale = 1.0 + medium_cols * (value_factor[:, :, None] - 1.0)
    return (noise * column_spread(head_scale) * shard_scale).astype(jnp.bfloat16)


def draw_grad_out(key, part):
    _, _, _, is_medium = decay_plan(key)
    _, grad_factor = shard_factors(key)
    noise = unit_noise(jax.random.fold_in(key, 7005), (BATCH_SEQUENCES, SEQUENCE_LENGTH, LOCAL_HEADS * DH))
    medium_cols = column_spread(is_medium.astype(jnp.float32))
    shard_scale = 1.0 + medium_cols * (grad_factor[:, :, None] - 1.0)
    return (noise * shard_scale).astype(jnp.bfloat16)


def draw_log_decay(key, part):
    decay_rate, rate_spread, _, _ = decay_plan(key)
    key_list = jax.random.split(jax.random.fold_in(key, 7003), 4)
    shard_count = SEQUENCE_LENGTH // TOK_DEV
    device_factor = jnp.exp(rate_spread[..., None] * jax.random.uniform(key_list[0], (BATCH_SEQUENCES, LOCAL_HEADS, shard_count, 1), jnp.float32, -1.0, 1.0))
    device_factor = jnp.broadcast_to(device_factor, (BATCH_SEQUENCES, LOCAL_HEADS, shard_count, TOK_DEV)).reshape(BATCH_SEQUENCES, LOCAL_HEADS, SEQUENCE_LENGTH)
    token_factor = jax.random.uniform(key_list[1], (BATCH_SEQUENCES, LOCAL_HEADS, SEQUENCE_LENGTH), jnp.float32, 0.5, 1.5)
    token_positions = jax.random.randint(key_list[2], (BATCH_SEQUENCES, 1, 3), 0, SEQUENCE_LENGTH)
    loss_values = jax.random.uniform(key_list[3], (BATCH_SEQUENCES, LOCAL_HEADS, 3), jnp.float32, 0.2, 0.5)
    shard_places = jnp.arange(SEQUENCE_LENGTH)[None, None, :]
    spike_record = jnp.zeros((BATCH_SEQUENCES, LOCAL_HEADS, SEQUENCE_LENGTH), jnp.float32)
    for spike_index in range(3):
        spike_record = spike_record + jnp.where(shard_places == token_positions[:, :, spike_index:spike_index + 1], jnp.log(1.0 - loss_values[:, :, spike_index:spike_index + 1]), 0.0)
    return jnp.maximum(-(decay_rate * device_factor * token_factor) + spike_record, -2.0)


def levels(key, extent, cuts, least, top_value):
    factor_of = 1.0
    for dim, blocks in cuts:
        steps = jax.random.uniform(jax.random.fold_in(jax.random.fold_in(key, 6), dim), (blocks,), jnp.float32, least / len(cuts), top_value / len(cuts))
        factor_of = factor_of * jnp.repeat(jnp.exp(steps), extent[dim] // blocks).reshape((-1,) + (1,) * (len(extent) - 1 - dim))
    return factor_of


def normal_values(own_key, shape, scale, bound, cuts=(), kind=jnp.bfloat16):
    result = jax.random.normal(own_key, shape, jnp.float32) * scale
    if len(cuts) > 0:
        result = levels(own_key, shape, cuts, -0.22, 0.18) * result
    return jnp.clip(result, min=-bound, max=bound).astype(kind)


def setup_inputs(seed: int = 0) -> dict:
    key_of = jax.random.split(jax.random.key(seed), 8)
    query = normal_values(key_of[0], (BATCH_SEQUENCES, SEQUENCE_LENGTH, LOCAL_HEADS * DH), 1.0, 6.0, ((0, 4), (1, 64)))
    key = normal_values(key_of[1], (BATCH_SEQUENCES, SEQUENCE_LENGTH, LOCAL_HEADS * DH), 1.0, 6.0, ((0, 4), (1, 64)))
    value = draw_value(jax.random.fold_in(key_of[7], 71), 0)
    log_decay = draw_log_decay(jax.random.fold_in(key_of[7], 71), 0)
    grad_out = draw_grad_out(jax.random.fold_in(key_of[7], 71), 0)
    query_map = normal_values(key_of[5], (LOCAL_HEADS, DH, DH), DH ** -0.5, 0.5)
    key_map = normal_values(key_of[6], (LOCAL_HEADS, DH, DH), DH ** -0.5, 0.5)
    return dict(query=query, key=key, value=value, log_decay=log_decay, grad_out=grad_out, query_map=query_map, key_map=key_map)


def silu_slope(pre_act):
    sigmoid_val = jax.nn.sigmoid(pre_act)
    return sigmoid_val * (1.0 + pre_act * (1.0 - sigmoid_val))

def feature_map(inputs, weight, block_len):
    head_count, head_width = (weight.shape[0], weight.shape[1])
    split_in = inputs.reshape(inputs.shape[0], head_count, head_width)
    pre_act = jnp.einsum('lhd,hde->hle', split_in.astype(jnp.float32), weight.astype(jnp.float32))
    features_out = jax.nn.silu(pre_act).astype(jnp.bfloat16)
    return (pre_act, features_out.reshape(head_count, -1, block_len, head_width))

def heads_blocks(array, head_count, block_len):
    rows = array.shape[0]
    return array.reshape(rows // block_len, block_len, head_count, -1).transpose(2, 0, 1, 3)

def unblock(array):
    head_count, block_count, block_len, head_width = array.shape
    return array.transpose(1, 2, 0, 3).reshape(block_count * block_len, head_count * head_width)

def chain_states(totals, updates):

    def advance(state, pieces):
        total_now, update_now = pieces
        return (jnp.exp(total_now)[:, None, None] * state + update_now, state)
    start = jnp.zeros((updates.shape[0], updates.shape[2], updates.shape[3]), jnp.float32)
    _, stacked = lax.scan(advance, start, (totals.T, updates.transpose(1, 0, 2, 3)))
    return stacked.transpose(1, 0, 2, 3)

def chain_adjoints(totals, contribs):

    def retreat(adjoint, pieces):
        total_now, contrib_now = pieces
        return (contrib_now + jnp.exp(total_now)[:, None, None] * adjoint, adjoint)
    start = jnp.zeros((contribs.shape[0], contribs.shape[2], contribs.shape[3]), jnp.float32)
    _, stacked = lax.scan(retreat, start, (totals.T, contribs.transpose(1, 0, 2, 3)), reverse=True)
    return stacked.transpose(1, 0, 2, 3)

def one_sequence(query_map, key_map, pieces):
    query, key, value, log_decay, grad_out = pieces
    head_count, head_width = (query_map.shape[0], query_map.shape[1])
    tokens = query.shape[0]
    out_scale = 1.0 / (head_width * math.sqrt(BLOCK))
    pre_query, query_feat = feature_map(query, query_map, BLOCK)
    pre_key, key_feat = feature_map(key, key_map, BLOCK)
    value_heads = heads_blocks(value, head_count, BLOCK)
    grad_heads = heads_blocks(grad_out, head_count, BLOCK)
    cumulative = jnp.cumsum(log_decay.reshape(head_count, -1, BLOCK), axis=-1)
    totals = cumulative[..., -1]
    causal_mask = jnp.arange(BLOCK)[:, None] >= jnp.arange(BLOCK)[None, :]
    differ = cumulative[..., :, None] - cumulative[..., None, :]
    weights = jnp.where(causal_mask, jnp.exp(jnp.where(causal_mask, differ, 0.0)), 0.0)
    query_wide = query_feat.astype(jnp.float32)
    key_wide = key_feat.astype(jnp.float32)
    value_wide = value_heads.astype(jnp.float32)
    grad_wide = grad_heads.astype(jnp.float32)
    scores = jnp.einsum('hnsd,hntd->hnst', query_wide, key_wide)
    block_probs = (scores * weights).astype(jnp.bfloat16)
    intra_out = jnp.einsum('hnst,hntd->hnsd', block_probs.astype(jnp.float32), value_wide)
    key_dec = (key_wide * jnp.exp(totals[..., None] - cumulative)[..., None]).astype(jnp.bfloat16)
    query_dec = (query_wide * jnp.exp(cumulative)[..., None]).astype(jnp.bfloat16)
    updates = jnp.einsum('hntd,hnte->hnde', key_dec.astype(jnp.float32), value_wide)
    state_round = chain_states(totals, updates).astype(jnp.bfloat16).astype(jnp.float32)
    inter_out = jnp.einsum('hnsd,hnde->hnse', query_dec.astype(jnp.float32), state_round)
    output = (out_scale * (intra_out + inter_out)).astype(jnp.bfloat16)
    contribs = jnp.einsum('hnsd,hnse->hnde', query_dec.astype(jnp.float32), grad_wide)
    after_round = chain_adjoints(totals, contribs).astype(jnp.bfloat16).astype(jnp.float32)
    grad_scores = (jnp.einsum('hnse,hnte->hnst', grad_wide, value_wide) * weights).astype(jnp.bfloat16)
    score_wide = grad_scores.astype(jnp.float32)
    grad_value = out_scale * (jnp.einsum('hnst,hnsd->hntd', block_probs.astype(jnp.float32), grad_wide) + jnp.einsum('hntd,hnde->hnte', key_dec.astype(jnp.float32), after_round))
    grad_qfeat = out_scale * (jnp.einsum('hnst,hntd->hnsd', score_wide, key_wide) + jnp.exp(cumulative)[..., None] * jnp.einsum('hnse,hnde->hnsd', grad_wide, state_round))
    grad_kfeat = out_scale * (jnp.einsum('hnst,hnsd->hntd', score_wide, query_wide) + jnp.exp(totals[..., None] - cumulative)[..., None] * jnp.einsum('hnte,hnde->hntd', value_wide, after_round))
    grad_pre_query = (grad_qfeat.reshape(head_count, tokens, head_width) * silu_slope(pre_query)).astype(jnp.bfloat16)
    grad_pre_key = (grad_kfeat.reshape(head_count, tokens, head_width) * silu_slope(pre_key)).astype(jnp.bfloat16)
    grad_query = jnp.einsum('hle,hde->lhd', grad_pre_query.astype(jnp.float32), query_map.astype(jnp.float32)).astype(jnp.bfloat16)
    grad_key = jnp.einsum('hle,hde->lhd', grad_pre_key.astype(jnp.float32), key_map.astype(jnp.float32)).astype(jnp.bfloat16)
    query_part = jnp.einsum('lhd,hle->hde', query.reshape(tokens, head_count, head_width).astype(jnp.float32), grad_pre_query.astype(jnp.float32))
    key_part = jnp.einsum('lhd,hle->hde', key.reshape(tokens, head_count, head_width).astype(jnp.float32), grad_pre_key.astype(jnp.float32))
    return (unblock(output), grad_query.reshape(tokens, -1), grad_key.reshape(tokens, -1), unblock(grad_value.astype(jnp.bfloat16)), query_part, key_part)

def reference(query, key, value, log_decay, grad_out, query_map, key_map):

    def per_sequence(pieces):
        return one_sequence(query_map, key_map, pieces)
    results = lax.map(per_sequence, (query, key, value, log_decay, grad_out))
    return (results[0], results[1], results[2], results[3], lax.optimization_barrier(jnp.sum(results[4], axis=0)), lax.optimization_barrier(jnp.sum(results[5], axis=0)))
```

```python
import math

import jax
import jax.numpy as jnp
from jax import lax
from jax.experimental import pallas as pl
from jax.experimental.pallas import tpu as pltpu
from jax.sharding import Mesh, PartitionSpec as P

BLOCK = 256
HEADS = 8
DH = 128
TOK = 512
HPB = 2
SCALE = 1.0 / (DH * math.sqrt(BLOCK))
F32 = jnp.float32
BF16 = jnp.bfloat16
CHIPS = 32
ROWS = HEADS * DH // CHIPS


def dot(a, b, dims=((1,), (0,))):
    return lax.dot_general(a, b, (dims, ((), ())), preferred_element_type=F32)


NT = ((1,), (1,))
TN = ((0,), (0,))


def split3(x):
    hi = x.astype(BF16)
    rest = x - hi.astype(F32)
    mid = rest.astype(BF16)
    low = (rest - mid.astype(F32)).astype(BF16)
    return jnp.concatenate([hi, mid, low], axis=1)


def lower3():
    t = lax.broadcasted_iota(jnp.int32, (BLOCK, BLOCK), 0)
    s = lax.broadcasted_iota(jnp.int32, (BLOCK, BLOCK), 1)
    low = jnp.where(s <= t, 1.0, 0.0).astype(BF16)
    return jnp.concatenate([low, low, low], axis=1)


def cumul_cols(low, row):
    return dot(low, split3(jnp.broadcast_to(row, (DH, BLOCK))), NT)


def cumul_rows(low, row):
    return dot(split3(jnp.broadcast_to(row, (8, BLOCK))), low, NT)


def sigmoid(u):
    return 1.0 / (1.0 + jnp.exp(-u))


def k1_body(core, q_ref, k_ref, v_ref, g_ref, ld_ref, wq_ref, wk_ref,
            qf_ref, kf_ref, mine_ref, send_ref, up_ref, con_ref, dec_ref):
    step = pl.program_id(0)
    first = core[0] == 0
    low = lower3()
    for i in range(HPB):
        lanes = slice(i * DH, (i + 1) * DH)
        ups, cons, tots = [], [], []
        for b in range(2):
            rows = slice(b * BLOCK, (b + 1) * BLOCK)
            row = ld_ref[pl.ds(step * HPB + i, 1), rows]
            cum = cumul_cols(low, row)
            tot = cum[BLOCK - 1:BLOCK, :]
            pre_q = dot(q_ref[rows, lanes], wq_ref[i])
            pre_k = dot(k_ref[rows, lanes], wk_ref[i])
            qf = (pre_q * sigmoid(pre_q)).astype(BF16)
            kf = (pre_k * sigmoid(pre_k)).astype(BF16)
            qf_ref[rows, lanes] = qf
            kf_ref[rows, lanes] = kf
            qdec = (qf.astype(F32) * jnp.exp(cum)).astype(BF16)
            kdec = (kf.astype(F32) * jnp.exp(tot - cum)).astype(BF16)
            ups.append(dot(kdec, v_ref[rows, lanes], TN))
            cons.append(dot(qdec, g_ref[rows, lanes], TN))
            tots.append(tot)
        d0, d1 = jnp.exp(tots[0]), jnp.exp(tots[1])
        up = d1 * ups[0] + ups[1]
        con = cons[0] + d0 * cons[1]
        mine_ref[i, 0:DH, :] = jnp.where(first, up, con)
        send_ref[i, 0:DH, :] = jnp.where(first, con, up)
        both = jnp.broadcast_to(d0 * d1, (8, DH))
        mine_ref[i, DH:DH + 8, :] = both
        send_ref[i, DH:DH + 8, :] = both
        up_ref[i] = ups[0]
        con_ref[i] = cons[1]
        dec_ref[i, 0:8, :] = jnp.broadcast_to(d0, (8, DH))
        dec_ref[i, 8:16, :] = jnp.broadcast_to(d1, (8, DH))


def combine_body(mine_ref, recv_ref, out_ref):
    for h in range(HEADS):
        other = recv_ref[h, DH:DH + 1, :]
        agg = other * mine_ref[h, 0:DH, :] + recv_ref[h, 0:DH, :]
        both = other * mine_ref[h, DH:DH + 1, :]
        for part in range(DH // ROWS):
            at = (h * (DH // ROWS) + part) * (ROWS + 1)
            out_ref[at:at + ROWS, :] = agg[part * ROWS:(part + 1) * ROWS, :]
            out_ref[at + ROWS:at + ROWS + 1, :] = both


def scan_body(core, in_ref, out_ref):
    first = core[0] == 0

    def pieces(k):
        at = k * (ROWS + 1)
        return in_ref[at:at + ROWS, :], in_ref[at + ROWS:at + ROWS + 1, :]

    state = jnp.zeros((ROWS, DH), F32)
    for k in range(CHIPS):
        out_ref[k * ROWS:(k + 1) * ROWS, :] = state
        part, decay = pieces(k)
        state = decay * state + part
    state = jnp.zeros((ROWS, DH), F32)
    for k in range(CHIPS - 1, -1, -1):
        rows = slice(k * ROWS, (k + 1) * ROWS)
        out_ref[rows, :] = jnp.where(first, out_ref[rows, :], state)
        part, decay = pieces(k)
        state = decay * state + part


def k2_body(q_ref, k_ref, v_ref, g_ref, ld_ref, wq_ref, wk_ref, qf_ref, kf_ref,
            aq_ref, bq_ref, ak_ref, bk_ref, oi_ref, vi_ref, qd_ref, kd_ref):
    step = pl.program_id(0)
    low = lower3()
    t = lax.broadcasted_iota(jnp.int32, (BLOCK, BLOCK), 0)
    s = lax.broadcasted_iota(jnp.int32, (BLOCK, BLOCK), 1)
    causal = s <= t
    for i in range(HPB):
        lanes = slice(i * DH, (i + 1) * DH)
        for b in range(2):
            rows = slice(b * BLOCK, (b + 1) * BLOCK)
            row = ld_ref[pl.ds(step * HPB + i, 1), rows]
            cum = cumul_cols(low, row)
            across = cumul_rows(low, row)[0:1, :]
            tot = cum[BLOCK - 1:BLOCK, :]
            wide = jnp.concatenate([cum, cum], axis=1)
            weights = jnp.exp(jnp.where(causal, wide - across, -1e9))
            qf, kf = qf_ref[rows, lanes], kf_ref[rows, lanes]
            v, g = v_ref[rows, lanes], g_ref[rows, lanes]
            probs = (dot(qf, kf, NT) * weights).astype(BF16)
            grads = (dot(g, v, NT) * weights).astype(BF16)
            oi_ref[rows, lanes] = SCALE * dot(probs, v)
            vi_ref[rows, lanes] = SCALE * dot(probs, g, TN)
            early, late = jnp.exp(cum), jnp.exp(tot - cum)
            qd_ref[rows, lanes] = (qf.astype(F32) * early).astype(BF16)
            kd_ref[rows, lanes] = (kf.astype(F32) * late).astype(BF16)
            pre_q = dot(q_ref[rows, lanes], wq_ref[i])
            sig_q = sigmoid(pre_q)
            slope_q = SCALE * (sig_q * (1.0 + pre_q * (1.0 - sig_q)))
            aq_ref[rows, lanes] = dot(grads, kf) * slope_q
            bq_ref[rows, lanes] = early * slope_q
            pre_k = dot(k_ref[rows, lanes], wk_ref[i])
            sig_k = sigmoid(pre_k)
            slope_k = SCALE * (sig_k * (1.0 + pre_k * (1.0 - sig_k)))
            ak_ref[rows, lanes] = dot(grads, qf, TN) * slope_k
            bk_ref[rows, lanes] = late * slope_k


def k3a_body(core, inc_ref, recv_ref, up_ref, con_ref, dec_ref, q_ref, k_ref, v_ref, g_ref,
             aq_ref, bq_ref, ak_ref, bk_ref,
             gpq_ref, gpk_ref, st_ref, af_ref, mine_ref, send_ref):
    first = core[0] == 0
    for i in range(HPB):
        lanes = slice(i * DH, (i + 1) * DH)
        inc, recv = inc_ref[i], recv_ref[i]
        state = jnp.where(first, inc, recv)
        after = jnp.where(first, recv, inc)
        d0, d1 = dec_ref[i, 0:1, :], dec_ref[i, 8:9, :]
        states = [state.astype(BF16), (d0 * state + up_ref[i]).astype(BF16)]
        afters = [(con_ref[i] + d1 * after).astype(BF16), after.astype(BF16)]
        for b in range(2):
            rows = slice(b * BLOCK, (b + 1) * BLOCK)
            st_ref[i, b] = states[b]
            af_ref[i, b] = afters[b]
            gpq_ref[rows, lanes] = (
                aq_ref[rows, lanes] + bq_ref[rows, lanes] * dot(g_ref[rows, lanes], states[b], NT)
            ).astype(BF16)
            gpk_ref[rows, lanes] = (
                ak_ref[rows, lanes] + bk_ref[rows, lanes] * dot(v_ref[rows, lanes], afters[b], NT)
            ).astype(BF16)
        part_q = dot(q_ref[:, lanes], gpq_ref[:, lanes], TN)
        part_k = dot(k_ref[:, lanes], gpk_ref[:, lanes], TN)
        mine_ref[i] = jnp.where(first, part_q, part_k)
        send_ref[i] = jnp.where(first, part_k, part_q)


def k3b_body(oi_ref, vi_ref, qd_ref, kd_ref, st_ref, af_ref, gpq_ref, gpk_ref, wq_ref, wk_ref,
             out_ref, gq_ref, gk_ref, gv_ref):
    for i in range(HPB):
        lanes = slice(i * DH, (i + 1) * DH)
        for b in range(2):
            rows = slice(b * BLOCK, (b + 1) * BLOCK)
            out_ref[rows, lanes] = (
                oi_ref[rows, lanes] + SCALE * dot(qd_ref[rows, lanes], st_ref[i, b])
            ).astype(BF16)
            gv_ref[rows, lanes] = (
                vi_ref[rows, lanes] + SCALE * dot(kd_ref[rows, lanes], af_ref[i, b])
            ).astype(BF16)
            gq_ref[rows, lanes] = dot(gpq_ref[rows, lanes], wq_ref[i], NT).astype(BF16)
            gk_ref[rows, lanes] = dot(gpk_ref[rows, lanes], wk_ref[i], NT).astype(BF16)


def spread_body(in_ref, out_ref):
    total = in_ref[0]
    for k in range(1, in_ref.shape[0]):
        total = total + in_ref[k]
    for k in range(out_ref.shape[0]):
        out_ref[k] = total


def add_body(a_ref, b_ref, out_ref):
    out_ref[...] = a_ref[...] + b_ref[...]


def smem():
    return pl.BlockSpec(memory_space=pltpu.SMEM)


def seq():
    return pl.BlockSpec((TOK, HPB * DH), lambda i: (0, i))


def per_head(*tail):
    zeros = (0,) * len(tail)
    return pl.BlockSpec((HPB,) + tail, lambda i: (i,) + zeros)


def whole(*shape):
    zeros = (0,) * len(shape)
    return pl.BlockSpec(shape, lambda i: zeros)


def shape(dims, kind=F32):
    return jax.ShapeDtypeStruct(dims, kind)


def call(body, name, ins, outs, out_shapes, flops=0, grid=HEADS // HPB, after=0):
    return pl.pallas_call(
        lambda *refs: body(*refs[after:]),
        grid=(grid,),
        in_specs=[pl.BlockSpec(memory_space=pl.ANY)] * after + ins,
        out_specs=outs,
        out_shape=out_shapes,
        name=name,
        cost_estimate=pl.CostEstimate(flops=flops, transcendentals=0, bytes_accessed=1 << 20),
        compiler_params=pltpu.CompilerParams(dimension_semantics=("arbitrary",)),
    )


def exchange(x, axes):
    return lax.all_to_all(x, axes, 0, 0, tiled=True)


def swap_cores(x):
    return lax.ppermute(x, "c", [(0, 1), (1, 0)])


SEQ_B = shape((TOK, HEADS * DH), BF16)
SEQ_F = shape((TOK, HEADS * DH), F32)
MAT = shape((HEADS, DH, DH), F32)


def local(query, key, value, log_decay, grad_out, query_map, key_map):
    core = lax.axis_index("c").astype(jnp.int32).reshape(1)
    q, k, v, g = (a[0] for a in (query, key, value, grad_out))
    ld = log_decay[0]
    maps = (query_map, key_map)
    seqs = (q, k, v, g)
    ld_spec = whole(HEADS, TOK)
    map_specs = [per_head(DH, DH)] * 2
    qf, kf, mine, send, up0, con1, dec = call(
        k1_body, "k1",
        [smem()] + [seq()] * 4 + [ld_spec] + map_specs,
        [seq(), seq(), per_head(DH + 8, DH), per_head(DH + 8, DH),
         per_head(DH, DH), per_head(DH, DH), per_head(16, DH)],
        [SEQ_B, SEQ_B, shape((HEADS, DH + 8, DH)), shape((HEADS, DH + 8, DH)), MAT, MAT,
         shape((HEADS, 16, DH))],
    )(core, *seqs, ld, *maps)
    recv = swap_cores(send)
    packed = call(
        combine_body, "combine",
        [whole(HEADS, DH + 8, DH)] * 2, whole(CHIPS * (ROWS + 1), DH),
        shape((CHIPS * (ROWS + 1), DH)), grid=1,
    )(mine, recv)
    swapped = exchange(packed.reshape(CHIPS, (ROWS + 1) * DH), ("z", "x"))
    aq, bq, ak, bk, oi, vi, qd, kd = call(
        k2_body, "k2",
        [seq()] * 4 + [ld_spec] + map_specs + [seq()] * 2,
        [seq()] * 8,
        [SEQ_F] * 6 + [SEQ_B] * 2,
        flops=1 << 30,
        after=1,
    )(packed, *seqs, ld, *maps, qf, kf)
    scanned = call(
        scan_body, "scan",
        [smem(), whole(CHIPS * (ROWS + 1), DH)], whole(CHIPS * ROWS, DH),
        shape((CHIPS * ROWS, DH)), grid=1, after=1,
    )(qd, core, swapped.reshape(CHIPS * (ROWS + 1), DH))
    inc = exchange(scanned.reshape(CHIPS, ROWS * DH), ("z", "x")).reshape(HEADS, DH, DH)
    passed = mine[:, DH:DH + 1, :] * inc + mine[:, :DH, :]
    recv = swap_cores(passed)
    gpq, gpk, st, af, mine, send = call(
        k3a_body, "k3a",
        [smem()] + [per_head(DH, DH)] * 4 + [per_head(16, DH)] + [seq()] * 8,
        [seq(), seq(), per_head(2, DH, DH), per_head(2, DH, DH), per_head(DH, DH), per_head(DH, DH)],
        [SEQ_B, SEQ_B, shape((HEADS, 2, DH, DH), BF16), shape((HEADS, 2, DH, DH), BF16), MAT, MAT],
    )(core, inc, recv, up0, con1, dec, *seqs, aq, bq, ak, bk)
    recv = swap_cores(send)
    chip = call(add_body, "add", [whole(HEADS, DH, DH)] * 2, whole(HEADS, DH, DH), MAT, grid=1)(
        mine, recv
    )
    pieces = exchange(chip.reshape(16, -1), ("x", "dp"))
    rows = HEADS * DH // 16
    out, gq, gk, gv = call(
        k3b_body, "k3b",
        [seq()] * 4 + [per_head(2, DH, DH)] * 2 + [seq()] * 2 + map_specs,
        [seq()] * 4,
        [SEQ_B] * 4,
        flops=1 << 30,
        after=1,
    )(chip, oi, vi, qd, kd, st, af, gpq, gpk, *maps)
    spread = call(spread_body, "spread_z", [whole(16, rows, DH)], whole(8, rows, DH),
                  shape((8, rows, DH)), grid=1, after=1)(out, pieces.reshape(16, rows, DH))
    pieces = exchange(spread.reshape(8, -1), "z")
    spread = call(spread_body, "spread_xy", [whole(8, rows, DH)], whole(16, rows, DH),
                  shape((16, rows, DH)), grid=1)(pieces.reshape(8, rows, DH))
    own = exchange(spread.reshape(16, -1), ("x", "dp")).reshape(HEADS, DH, DH)
    other = swap_cores(own)
    first = core[0] == 0
    query_map_grad = jnp.where(first, own, other)
    key_map_grad = jnp.where(first, other, own)
    return (out[None], gq[None], gk[None], gv[None], query_map_grad, key_map_grad)


def solution(mesh):
    fine = Mesh(mesh.devices.reshape(8, 4, 2, 4), ("z", "x", "c", "dp"))
    ctx = ("z", "x", "c")
    act = P("dp", ctx, None)
    return jax.shard_map(
        local,
        mesh=fine,
        in_specs=(act, act, act, P("dp", None, ctx), act, P(), P()),
        out_specs=(act, act, act, act, P(), P()),
        check_vma=False,
    )
```

```python
import math

import jax
import jax.numpy as jnp
from jax import lax
from jax.experimental import pallas as pl
from jax.experimental.pallas import tpu as pltpu
from jax.sharding import Mesh, PartitionSpec as P

BLOCK = 256
HEADS = 8
DH = 128
TOK = 512
HPB = 2
SCALE = 1.0 / (DH * math.sqrt(BLOCK))
F32 = jnp.float32
BF16 = jnp.bfloat16
CHIPS = 32
ROWS = HEADS * DH // CHIPS


def dot(a, b, dims=((1,), (0,))):
    return lax.dot_general(a, b, (dims, ((), ())), preferred_element_type=F32)


NT = ((1,), (1,))
TN = ((0,), (0,))


def split3(x):
    hi = x.astype(BF16)
    rest = x - hi.astype(F32)
    mid = rest.astype(BF16)
    low = (rest - mid.astype(F32)).astype(BF16)
    return jnp.concatenate([hi, mid, low], axis=1)


def lower3():
    t = lax.broadcasted_iota(jnp.int32, (BLOCK, BLOCK), 0)
    s = lax.broadcasted_iota(jnp.int32, (BLOCK, BLOCK), 1)
    low = jnp.where(s <= t, 1.0, 0.0).astype(BF16)
    return jnp.concatenate([low, low, low], axis=1)


def cumul_cols(low, row):
    return dot(low, split3(jnp.broadcast_to(row, (DH, BLOCK))), NT)


def cumul_rows(low, rows):
    return dot(split3(rows), low, NT)


def sigmoid(u):
    return 1.0 / (1.0 + jnp.exp(-u))


def k1_body(core, q_ref, k_ref, v_ref, g_ref, ld_ref, wq_ref, wk_ref,
            mine_ref, send_ref, up_ref, con_ref, dec_ref, cum_ref):
    step = pl.program_id(0)
    first = core[0] == 0

    @pl.when(step == 0)
    def _():
        low = lower3()
        for b in range(2):
            rows = slice(b * BLOCK, (b + 1) * BLOCK)
            cum_ref[:, rows] = cumul_rows(low, ld_ref[:, rows])

    for i in range(HPB):
        lanes = slice(i * DH, (i + 1) * DH)
        ups, cons, tots = [], [], []
        for b in range(2):
            rows = slice(b * BLOCK, (b + 1) * BLOCK)
            cum = cum_ref[pl.ds(step * HPB + i, 1), rows]
            tot = cum[:, BLOCK - 1:BLOCK]
            pre_q = dot(wq_ref[i], q_ref[rows, lanes], ((0,), (1,)))
            pre_k = dot(wk_ref[i], k_ref[rows, lanes], ((0,), (1,)))
            qf = (pre_q * sigmoid(pre_q)).astype(BF16)
            kf = (pre_k * sigmoid(pre_k)).astype(BF16)
            qdec = (qf.astype(F32) * jnp.exp(cum)).astype(BF16)
            kdec = (kf.astype(F32) * jnp.exp(tot - cum)).astype(BF16)
            ups.append(dot(kdec, v_ref[rows, lanes]))
            cons.append(dot(qdec, g_ref[rows, lanes]))
            tots.append(jnp.broadcast_to(tot, (8, DH)))
        d0, d1 = jnp.exp(tots[0]), jnp.exp(tots[1])
        up = d1[0:1] * ups[0] + ups[1]
        con = cons[0] + d0[0:1] * cons[1]
        mine_ref[i, 0:DH, :] = jnp.where(first, up, con)
        send_ref[i, 0:DH, :] = jnp.where(first, con, up)
        mine_ref[i, DH:DH + 8, :] = d0 * d1
        send_ref[i, DH:DH + 8, :] = d0 * d1
        up_ref[i] = ups[0]
        con_ref[i] = cons[1]
        dec_ref[i, 0:8, :] = d0
        dec_ref[i, 8:16, :] = d1


def combine_body(mine_ref, recv_ref, out_ref):
    for h in range(HEADS):
        other = recv_ref[h, DH:DH + 1, :]
        agg = other * mine_ref[h, 0:DH, :] + recv_ref[h, 0:DH, :]
        both = other * mine_ref[h, DH:DH + 1, :]
        for part in range(DH // ROWS):
            at = (h * (DH // ROWS) + part) * (ROWS + 1)
            out_ref[at:at + ROWS, :] = agg[part * ROWS:(part + 1) * ROWS, :]
            out_ref[at + ROWS:at + ROWS + 1, :] = both


def scan_body(core, in_ref, out_ref):
    first = core[0] == 0

    def pieces(k):
        at = k * (ROWS + 1)
        return in_ref[at:at + ROWS, :], in_ref[at + ROWS:at + ROWS + 1, :]

    state = jnp.zeros((ROWS, DH), F32)
    for k in range(CHIPS):
        out_ref[k * ROWS:(k + 1) * ROWS, :] = state
        part, decay = pieces(k)
        state = decay * state + part
    state = jnp.zeros((ROWS, DH), F32)
    for k in range(CHIPS - 1, -1, -1):
        rows = slice(k * ROWS, (k + 1) * ROWS)
        out_ref[rows, :] = jnp.where(first, out_ref[rows, :], state)
        part, decay = pieces(k)
        state = decay * state + part


def k2_body(q_ref, k_ref, v_ref, g_ref, ld_ref, wq_ref, wk_ref,
            aq_ref, bq_ref, ak_ref, bk_ref, oi_ref, vi_ref, qd_ref, kd_ref, qt_ref, kt_ref,
            mark_ref, low_ref, cum_ref):
    step = pl.program_id(0)

    @pl.when(step == 0)
    def _():
        low_ref[...] = lower3()
        for b in range(2):
            rows = slice(b * BLOCK, (b + 1) * BLOCK)
            cum_ref[:, rows] = cumul_rows(low_ref[...], ld_ref[:, rows])

    t = lax.broadcasted_iota(jnp.int32, (BLOCK, BLOCK), 0)
    s = lax.broadcasted_iota(jnp.int32, (BLOCK, BLOCK), 1)
    causal = s <= t
    for i in range(HPB):
        lanes = slice(i * DH, (i + 1) * DH)
        qt_ref[i] = q_ref[:, lanes].T
        kt_ref[i] = k_ref[:, lanes].T
        for b in range(2):
            rows = slice(b * BLOCK, (b + 1) * BLOCK)
            head = pl.ds(step * HPB + i, 1)
            cum = cumul_cols(low_ref[...], ld_ref[head, rows])
            across = cum_ref[head, rows]
            tot = cum[BLOCK - 1:BLOCK, :]
            wide = jnp.concatenate([cum, cum], axis=1)
            weights = jnp.exp(jnp.where(causal, wide - across, -1e9))
            v, g = v_ref[rows, lanes], g_ref[rows, lanes]
            pre_q = dot(q_ref[rows, lanes], wq_ref[i])
            pre_k = dot(k_ref[rows, lanes], wk_ref[i])
            sig_q, sig_k = sigmoid(pre_q), sigmoid(pre_k)
            qf, kf = (pre_q * sig_q).astype(BF16), (pre_k * sig_k).astype(BF16)
            probs = (dot(qf, kf, NT) * weights).astype(BF16)
            grads = (dot(g, v, NT) * weights).astype(BF16)
            oi_ref[rows, lanes] = SCALE * dot(probs, v)
            vi_ref[rows, lanes] = SCALE * dot(probs, g, TN)
            early, late = jnp.exp(cum), jnp.exp(tot - cum)
            qd_ref[rows, lanes] = (qf.astype(F32) * early).astype(BF16)
            kd_ref[rows, lanes] = (kf.astype(F32) * late).astype(BF16)
            slope_q = SCALE * (sig_q * (1.0 + pre_q * (1.0 - sig_q)))
            aq_ref[rows, lanes] = dot(grads, kf) * slope_q
            bq_ref[rows, lanes] = early * slope_q
            slope_k = SCALE * (sig_k * (1.0 + pre_k * (1.0 - sig_k)))
            ak_ref[rows, lanes] = dot(grads, qf, TN) * slope_k
            bk_ref[rows, lanes] = late * slope_k
    mark_ref[...] = jnp.zeros((8, DH), F32)


def k3a_body(core, inc_ref, recv_ref, up_ref, con_ref, dec_ref, qt_ref, kt_ref, v_ref, g_ref,
             aq_ref, bq_ref, ak_ref, bk_ref,
             gpq_ref, gpk_ref, st_ref, af_ref, mine_ref, send_ref):
    first = core[0] == 0
    for i in range(HPB):
        lanes = slice(i * DH, (i + 1) * DH)
        head = pl.program_id(0) * HPB + i
        inc, recv = inc_ref[head], recv_ref[head]
        state = jnp.where(first, inc, recv)
        after = jnp.where(first, recv, inc)
        d0, d1 = dec_ref[i, 0:1, :], dec_ref[i, 8:9, :]
        states = [state.astype(BF16), (d0 * state + up_ref[i]).astype(BF16)]
        afters = [(con_ref[i] + d1 * after).astype(BF16), after.astype(BF16)]
        for b in range(2):
            rows = slice(b * BLOCK, (b + 1) * BLOCK)
            st_ref[i, b] = states[b]
            af_ref[i, b] = afters[b]
            gpq_ref[rows, lanes] = (
                aq_ref[rows, lanes] + bq_ref[rows, lanes] * dot(g_ref[rows, lanes], states[b], NT)
            ).astype(BF16)
            gpk_ref[rows, lanes] = (
                ak_ref[rows, lanes] + bk_ref[rows, lanes] * dot(v_ref[rows, lanes], afters[b], NT)
            ).astype(BF16)
        part_q = dot(qt_ref[i], gpq_ref[:, lanes])
        part_k = dot(kt_ref[i], gpk_ref[:, lanes])
        mine_ref[i] = jnp.where(first, part_q, part_k)
        send_ref[i] = jnp.where(first, part_k, part_q)


def k3b_body(oi_ref, vi_ref, qd_ref, kd_ref, st_ref, af_ref, gpq_ref, gpk_ref, wq_ref, wk_ref,
             out_ref, gq_ref, gk_ref, gv_ref, mark_ref):
    mark_ref[...] = jnp.zeros((8, DH), F32)
    for i in range(HPB):
        lanes = slice(i * DH, (i + 1) * DH)
        for b in range(2):
            rows = slice(b * BLOCK, (b + 1) * BLOCK)
            out_ref[rows, lanes] = (
                oi_ref[rows, lanes] + SCALE * dot(qd_ref[rows, lanes], st_ref[i, b])
            ).astype(BF16)
            gv_ref[rows, lanes] = (
                vi_ref[rows, lanes] + SCALE * dot(kd_ref[rows, lanes], af_ref[i, b])
            ).astype(BF16)
            gq_ref[rows, lanes] = dot(gpq_ref[rows, lanes], wq_ref[i], NT).astype(BF16)
            gk_ref[rows, lanes] = dot(gpk_ref[rows, lanes], wk_ref[i], NT).astype(BF16)


def spread_body(in_ref, out_ref):
    total = in_ref[0]
    for k in range(1, in_ref.shape[0]):
        total = total + in_ref[k]
    for k in range(out_ref.shape[0]):
        out_ref[k] = total


def smem():
    return pl.BlockSpec(memory_space=pltpu.SMEM)


def seq():
    return pl.BlockSpec((TOK, HPB * DH), lambda i: (0, i))


def per_head(*tail):
    zeros = (0,) * len(tail)
    return pl.BlockSpec((HPB,) + tail, lambda i: (i,) + zeros)


def whole(*shape):
    zeros = (0,) * len(shape)
    return pl.BlockSpec(shape, lambda i: zeros)


def shape(dims, kind=F32):
    return jax.ShapeDtypeStruct(dims, kind)


def call(body, name, ins, outs, out_shapes, flops=0, grid=HEADS // HPB, after=0,
         scratch=(), grant=None):
    return pl.pallas_call(
        lambda *refs: body(*refs[after:]),
        grid=(grid,),
        in_specs=[pl.BlockSpec(memory_space=pl.ANY)] * after + ins,
        out_specs=outs,
        out_shape=out_shapes,
        scratch_shapes=scratch,
        name=name,
        cost_estimate=pl.CostEstimate(flops=flops, transcendentals=0, bytes_accessed=1 << 20),
        compiler_params=pltpu.CompilerParams(
            dimension_semantics=("arbitrary",), vmem_limit_bytes=grant
        ),
    )


def small(body, name, ins, out_shape, out_spec, smem=0, after=0):
    vmem = pl.BlockSpec(memory_space=pltpu.VMEM)
    return pl.pallas_call(
        lambda *refs: body(*refs[after:]),
        grid=(1,),
        in_specs=[pl.BlockSpec(memory_space=pl.ANY)] * after
        + [pl.BlockSpec(memory_space=pltpu.SMEM)] * smem + [vmem] * ins,
        out_specs=out_spec,
        out_shape=out_shape,
        name=name,
        compiler_params=pltpu.CompilerParams(vmem_limit_bytes=8 << 20),
    )


def exchange(x, axes):
    return lax.all_to_all(x, axes, 0, 0, tiled=True)


def swap_cores(x):
    return lax.ppermute(x, "c", [(0, 1), (1, 0)])


SEQ_B = shape((TOK, HEADS * DH), BF16)
SEQ_F = shape((TOK, HEADS * DH), F32)
MAT = shape((HEADS, DH, DH), F32)


def local(query, key, value, log_decay, grad_out, query_map, key_map):
    core = lax.axis_index("c").astype(jnp.int32).reshape(1)
    q, k, v, g = (a[0] for a in (query, key, value, grad_out))
    ld = log_decay[0]
    maps = (query_map, key_map)
    seqs = (q, k, v, g)
    ld_spec = whole(HEADS, TOK)
    map_specs = [per_head(DH, DH)] * 2
    mine, send, up0, con1, dec = call(
        k1_body, "k1",
        [smem()] + [seq()] * 4 + [ld_spec] + map_specs,
        [per_head(DH + 8, DH), per_head(DH + 8, DH),
         per_head(DH, DH), per_head(DH, DH), per_head(16, DH)],
        [shape((HEADS, DH + 8, DH)), shape((HEADS, DH + 8, DH)), MAT, MAT,
         shape((HEADS, 16, DH))],
        scratch=[pltpu.VMEM((HEADS, TOK), F32)],
    )(core, *seqs, ld, *maps)
    recv = swap_cores(send)
    packed = small(
        combine_body, "combine", 2, shape((CHIPS * (ROWS + 1), DH)), whole(CHIPS * (ROWS + 1), DH),
    )(mine, recv)
    swapped = exchange(packed.reshape(CHIPS, (ROWS + 1) * DH), ("z", "x"))
    aq, bq, ak, bk, oi, vi, qd, kd, qt, kt, mark = call(
        k2_body, "k2",
        [seq()] * 4 + [ld_spec] + map_specs,
        [seq()] * 8 + [per_head(DH, TOK)] * 2 + [whole(8, DH)],
        [SEQ_F] * 6 + [SEQ_B] * 2 + [shape((HEADS, DH, TOK), BF16)] * 2 + [shape((8, DH))],
        flops=1 << 30,
        after=1,
        scratch=[pltpu.VMEM((BLOCK, 3 * BLOCK), BF16), pltpu.VMEM((HEADS, TOK), F32)],
    )(packed, *seqs, ld, *maps)
    scanned = small(
        scan_body, "scan", 1, shape((CHIPS * ROWS, DH)), whole(CHIPS * ROWS, DH), smem=1, after=1,
    )(mark, core, swapped.reshape(CHIPS * (ROWS + 1), DH))
    inc = exchange(scanned.reshape(CHIPS, ROWS * DH), ("z", "x")).reshape(HEADS, DH, DH)
    passed = mine[:, DH:DH + 1, :] * inc + mine[:, :DH, :]
    recv = swap_cores(passed)
    gpq, gpk, st, af, mine, send = call(
        k3a_body, "k3a",
        [smem()] + [pl.BlockSpec(memory_space=pltpu.VMEM)] * 2 + [per_head(DH, DH)] * 2
        + [per_head(16, DH)] + [per_head(DH, TOK)] * 2 + [seq()] * 6,
        [seq(), seq(), per_head(2, DH, DH), per_head(2, DH, DH), per_head(DH, DH), per_head(DH, DH)],
        [SEQ_B, SEQ_B, shape((HEADS, 2, DH, DH), BF16), shape((HEADS, 2, DH, DH), BF16), MAT, MAT],
        grant=57 << 20,
    )(core, inc, recv, up0, con1, dec, qt, kt, v, g, aq, bq, ak, bk)
    recv = swap_cores(send)
    chip = mine + recv
    pieces = exchange(chip.reshape(16, -1), ("x", "dp"))
    rows = HEADS * DH // 16
    out, gq, gk, gv, mark = call(
        k3b_body, "k3b",
        [seq()] * 4 + [per_head(2, DH, DH)] * 2 + [seq()] * 2 + map_specs,
        [seq()] * 4 + [whole(8, DH)],
        [SEQ_B] * 4 + [shape((8, DH))],
        flops=1 << 30,
        after=1,
    )(chip, oi, vi, qd, kd, st, af, gpq, gpk, *maps)
    spread = small(spread_body, "spread_z", 1, shape((8, rows, DH)), whole(8, rows, DH), after=1)(
        mark, pieces.reshape(16, rows, DH)
    )
    pieces = exchange(spread.reshape(8, -1), "z")
    spread = small(spread_body, "spread_xy", 1, shape((16, rows, DH)), whole(16, rows, DH))(
        pieces.reshape(8, rows, DH)
    )
    own = exchange(spread.reshape(16, -1), ("x", "dp")).reshape(HEADS, DH, DH)
    other = swap_cores(own)
    first = core[0] == 0
    query_map_grad = jnp.where(first, own, other)
    key_map_grad = jnp.where(first, other, own)
    return (out[None], gq[None], gk[None], gv[None], query_map_grad, key_map_grad)


def solution(mesh):
    fine = Mesh(mesh.devices.reshape(8, 4, 2, 4), ("z", "x", "c", "dp"))
    ctx = ("z", "x", "c")
    act = P("dp", ctx, None)
    return jax.shard_map(
        local,
        mesh=fine,
        in_specs=(act, act, act, P("dp", None, ctx), act, P(), P()),
        out_specs=(act, act, act, act, P(), P()),
        check_vma=False,
    )
```

```python
import math

import jax
import jax.numpy as jnp
from jax import lax
from jax.experimental import pallas as pl
from jax.experimental.pallas import tpu as pltpu
from jax.sharding import Mesh, PartitionSpec as P

BLOCK = 256
HEADS = 8
DH = 128
TOK = 512
HPB = 2
SCALE = 1.0 / (DH * math.sqrt(BLOCK))
F32 = jnp.float32
BF16 = jnp.bfloat16
CHIPS = 32
ROWS = HEADS * DH // CHIPS


def dot(a, b, dims=((1,), (0,))):
    return lax.dot_general(a, b, (dims, ((), ())), preferred_element_type=F32)


NT = ((1,), (1,))
TN = ((0,), (0,))


def split3(x):
    hi = x.astype(BF16)
    rest = x - hi.astype(F32)
    mid = rest.astype(BF16)
    low = (rest - mid.astype(F32)).astype(BF16)
    return jnp.concatenate([hi, mid, low], axis=1)


def lower3():
    t = lax.broadcasted_iota(jnp.int32, (BLOCK, BLOCK), 0)
    s = lax.broadcasted_iota(jnp.int32, (BLOCK, BLOCK), 1)
    low = jnp.where(s <= t, 1.0, 0.0).astype(BF16)
    return jnp.concatenate([low, low, low], axis=1)


def cumul_cols(low, row):
    return dot(low, split3(jnp.broadcast_to(row, (DH, BLOCK))), NT)


def cumul_rows(low, rows):
    return dot(split3(rows), low, NT)


def sigmoid(u):
    return 1.0 / (1.0 + jnp.exp(-u))


def k1_body(core, q_ref, k_ref, v_ref, g_ref, ld_ref, wq_ref, wk_ref,
            mine_ref, send_ref, up_ref, con_ref, dec_ref, cum_ref):
    step = pl.program_id(0)
    first = core[0] == 0

    @pl.when(step == 0)
    def _():
        low = lower3()
        for b in range(2):
            rows = slice(b * BLOCK, (b + 1) * BLOCK)
            cum_ref[:, rows] = cumul_rows(low, ld_ref[:, rows])

    for i in range(HPB):
        lanes = slice(i * DH, (i + 1) * DH)
        ups, cons, tots = [], [], []
        for b in range(2):
            rows = slice(b * BLOCK, (b + 1) * BLOCK)
            cum = cum_ref[pl.ds(step * HPB + i, 1), rows]
            tot = cum[:, BLOCK - 1:BLOCK]
            pre_q = dot(wq_ref[i], q_ref[rows, lanes], ((0,), (1,)))
            pre_k = dot(wk_ref[i], k_ref[rows, lanes], ((0,), (1,)))
            qf = (pre_q * sigmoid(pre_q)).astype(BF16)
            kf = (pre_k * sigmoid(pre_k)).astype(BF16)
            qdec = (qf.astype(F32) * jnp.exp(cum)).astype(BF16)
            kdec = (kf.astype(F32) * jnp.exp(tot - cum)).astype(BF16)
            ups.append(dot(kdec, v_ref[rows, lanes]))
            cons.append(dot(qdec, g_ref[rows, lanes]))
            tots.append(jnp.broadcast_to(tot, (8, DH)))
        d0, d1 = jnp.exp(tots[0]), jnp.exp(tots[1])
        up = d1[0:1] * ups[0] + ups[1]
        con = cons[0] + d0[0:1] * cons[1]
        mine_ref[i, 0:DH, :] = jnp.where(first, up, con)
        send_ref[i, 0:DH, :] = jnp.where(first, con, up)
        mine_ref[i, DH:DH + 8, :] = d0 * d1
        send_ref[i, DH:DH + 8, :] = d0 * d1
        up_ref[i] = ups[0]
        con_ref[i] = cons[1]
        dec_ref[i, 0:8, :] = d0
        dec_ref[i, 8:16, :] = d1


def combine_body(mine_ref, recv_ref, out_ref):
    for h in range(HEADS):
        other = recv_ref[h, DH:DH + 1, :]
        agg = other * mine_ref[h, 0:DH, :] + recv_ref[h, 0:DH, :]
        both = other * mine_ref[h, DH:DH + 1, :]
        for part in range(DH // ROWS):
            at = (h * (DH // ROWS) + part) * (ROWS + 1)
            out_ref[at:at + ROWS, :] = agg[part * ROWS:(part + 1) * ROWS, :]
            out_ref[at + ROWS:at + ROWS + 1, :] = both


def scan_body(core, in_ref, out_ref):
    first = core[0] == 0

    def pieces(k):
        at = k * (ROWS + 1)
        return in_ref[at:at + ROWS, :], in_ref[at + ROWS:at + ROWS + 1, :]

    state = jnp.zeros((ROWS, DH), F32)
    for k in range(CHIPS):
        out_ref[k * ROWS:(k + 1) * ROWS, :] = state
        part, decay = pieces(k)
        state = decay * state + part
    state = jnp.zeros((ROWS, DH), F32)
    for k in range(CHIPS - 1, -1, -1):
        rows = slice(k * ROWS, (k + 1) * ROWS)
        out_ref[rows, :] = jnp.where(first, out_ref[rows, :], state)
        part, decay = pieces(k)
        state = decay * state + part


def k2_body(core, q_ref, k_ref, v_ref, g_ref, ld_ref, wq_ref, wk_ref,
            aq_ref, bq_ref, ak_ref, bk_ref, oi_ref, vi_ref, qd_ref, kd_ref, qt_ref, kt_ref,
            mark_ref, low_ref, cum_ref):
    step = pl.program_id(0)

    @pl.when(step == 0)
    def _():
        low_ref[...] = lower3()
        for b in range(2):
            rows = slice(b * BLOCK, (b + 1) * BLOCK)
            cum_ref[:, rows] = cumul_rows(low_ref[...], ld_ref[:, rows])

    t = lax.broadcasted_iota(jnp.int32, (BLOCK, BLOCK), 0)
    s = lax.broadcasted_iota(jnp.int32, (BLOCK, BLOCK), 1)
    causal = s <= t
    for i in range(HPB):
        lanes = slice(i * DH, (i + 1) * DH)
        qt_ref[i] = q_ref[:, lanes].T
        kt_ref[i] = k_ref[:, lanes].T
        for b in range(2):
            rows = slice(b * BLOCK, (b + 1) * BLOCK)
            head = pl.ds(step * HPB + i, 1)
            cum = cumul_cols(low_ref[...], ld_ref[head, rows])
            across = cum_ref[head, rows]
            tot = cum[BLOCK - 1:BLOCK, :]
            wide = jnp.concatenate([cum, cum], axis=1)
            weights = jnp.exp(jnp.where(causal, wide - across, -1e9))
            v, g = v_ref[rows, lanes], g_ref[rows, lanes]
            pre_q = dot(q_ref[rows, lanes], wq_ref[i])
            pre_k = dot(k_ref[rows, lanes], wk_ref[i])
            sig_q, sig_k = sigmoid(pre_q), sigmoid(pre_k)
            qf, kf = (pre_q * sig_q).astype(BF16), (pre_k * sig_k).astype(BF16)
            probs = (dot(qf, kf, NT) * weights).astype(BF16)
            grads = (dot(g, v, NT) * weights).astype(BF16)
            oi_ref[i, rows] = SCALE * dot(probs, v)
            vi_ref[i, rows] = SCALE * dot(probs, g, TN)
            early, late = jnp.exp(cum), jnp.exp(tot - cum)
            qd_ref[i, rows] = (qf.astype(F32) * early).astype(BF16)
            kd_ref[i, rows] = (kf.astype(F32) * late).astype(BF16)
            slope_q = SCALE * (sig_q * (1.0 + pre_q * (1.0 - sig_q)))
            aq_ref[i, rows] = (dot(grads, kf) * slope_q).astype(BF16)
            bq_ref[i, rows] = (early * slope_q).astype(BF16)
            slope_k = SCALE * (sig_k * (1.0 + pre_k * (1.0 - sig_k)))
            ak_ref[i, rows] = (dot(grads, qf, TN) * slope_k).astype(BF16)
            bk_ref[i, rows] = (late * slope_k).astype(BF16)
    mark_ref[0] = core[0]


def states_body(core, inc_ref, recv_ref, up_ref, con_ref, dec_ref, st_ref, af_ref):
    first = core[0] == 0
    for h in range(HEADS):
        inc, recv = inc_ref[h], recv_ref[h]
        state = jnp.where(first, inc, recv)
        after = jnp.where(first, recv, inc)
        st_ref[h, 0] = state.astype(BF16)
        st_ref[h, 1] = (dec_ref[h, 0:1, :] * state + up_ref[h]).astype(BF16)
        af_ref[h, 0] = (con_ref[h] + dec_ref[h, 8:9, :] * after).astype(BF16)
        af_ref[h, 1] = after.astype(BF16)


def k3a_body(core, st_ref, af_ref, qt_ref, kt_ref, v_ref, g_ref,
             aq_ref, bq_ref, ak_ref, bk_ref, gpq_ref, gpk_ref, mine_ref, send_ref):
    first = core[0] == 0
    for i in range(HPB):
        lanes = slice(i * DH, (i + 1) * DH)
        for b in range(2):
            rows = slice(b * BLOCK, (b + 1) * BLOCK)
            from_state = dot(g_ref[rows, lanes], st_ref[i, b], NT)
            from_after = dot(v_ref[rows, lanes], af_ref[i, b], NT)
            gpq_ref[i, rows] = (
                aq_ref[i, rows].astype(F32) + bq_ref[i, rows].astype(F32) * from_state
            ).astype(BF16)
            gpk_ref[i, rows] = (
                ak_ref[i, rows].astype(F32) + bk_ref[i, rows].astype(F32) * from_after
            ).astype(BF16)
        part_q = dot(qt_ref[i], gpq_ref[i])
        part_k = dot(kt_ref[i], gpk_ref[i])
        mine_ref[i] = jnp.where(first, part_q, part_k)
        send_ref[i] = jnp.where(first, part_k, part_q)


def k3b_body(core, oi_ref, vi_ref, qd_ref, kd_ref, st_ref, af_ref, gpq_ref, gpk_ref, wq_ref, wk_ref,
             out_ref, gq_ref, gk_ref, gv_ref, mark_ref):
    mark_ref[0] = core[0]
    for i in range(HPB):
        lanes = slice(i * DH, (i + 1) * DH)
        for b in range(2):
            rows = slice(b * BLOCK, (b + 1) * BLOCK)
            out_ref[rows, lanes] = (
                oi_ref[i, rows] + SCALE * dot(qd_ref[i, rows], st_ref[i, b])
            ).astype(BF16)
            gv_ref[rows, lanes] = (
                vi_ref[i, rows] + SCALE * dot(kd_ref[i, rows], af_ref[i, b])
            ).astype(BF16)
            gq_ref[rows, lanes] = dot(gpq_ref[i, rows], wq_ref[i], NT).astype(BF16)
            gk_ref[rows, lanes] = dot(gpk_ref[i, rows], wk_ref[i], NT).astype(BF16)


def add_body(a_ref, b_ref, out_ref):
    out_ref[...] = a_ref[...] + b_ref[...]


def spread_first_body(core, in_ref, out_ref):
    spread_body(in_ref, out_ref)


def spread_body(in_ref, out_ref):
    total = in_ref[0]
    for k in range(1, in_ref.shape[0]):
        total = total + in_ref[k]
    for k in range(out_ref.shape[0]):
        out_ref[k] = total


def smem():
    return pl.BlockSpec(memory_space=pltpu.SMEM)


def seq():
    return pl.BlockSpec((TOK, HPB * DH), lambda i: (0, i))


def per_head(*tail):
    zeros = (0,) * len(tail)
    return pl.BlockSpec((HPB,) + tail, lambda i: (i,) + zeros)


def whole(*shape):
    zeros = (0,) * len(shape)
    return pl.BlockSpec(shape, lambda i: zeros)


def shape(dims, kind=F32):
    return jax.ShapeDtypeStruct(dims, kind)


def call(body, name, ins, outs, out_shapes, flops=0, grid=HEADS // HPB, after=0,
         scratch=(), grant=None):
    return pl.pallas_call(
        lambda *refs: body(*refs[after:]),
        grid=(grid,),
        in_specs=[pl.BlockSpec(memory_space=pltpu.HBM)] * after + ins,
        out_specs=outs,
        out_shape=out_shapes,
        scratch_shapes=scratch,
        name=name,
        cost_estimate=pl.CostEstimate(flops=flops, transcendentals=0, bytes_accessed=1 << 20),
        compiler_params=pltpu.CompilerParams(
            dimension_semantics=("arbitrary",), vmem_limit_bytes=grant
        ),
    )


def small(body, name, ins, out_shape, out_spec, smem=0, after=0):
    vmem = pl.BlockSpec(memory_space=pltpu.VMEM)
    return pl.pallas_call(
        lambda *refs: body(*refs[after:]),
        grid=(1,),
        in_specs=[pl.BlockSpec(memory_space=pltpu.HBM)] * after
        + [pl.BlockSpec(memory_space=pltpu.SMEM)] * smem + [vmem] * ins,
        out_specs=out_spec,
        out_shape=out_shape,
        name=name,
        compiler_params=pltpu.CompilerParams(vmem_limit_bytes=8 << 20),
    )


def exchange(x, axes):
    return lax.all_to_all(x, axes, 0, 0, tiled=True)


def swap_cores(x):
    return lax.ppermute(x, "c", [(0, 1), (1, 0)])


SEQ_B = shape((TOK, HEADS * DH), BF16)
SEQ_F = shape((TOK, HEADS * DH), F32)
MAT = shape((HEADS, DH, DH), F32)
HELD_F = shape((HEADS, TOK, DH), F32)
HELD_B = shape((HEADS, TOK, DH), BF16)


def local(query, key, value, log_decay, grad_out, query_map, key_map):
    core = lax.axis_index("c").astype(jnp.int32).reshape(1)
    q, k, v, g = (a[0] for a in (query, key, value, grad_out))
    ld = log_decay[0]
    maps = (query_map, key_map)
    seqs = (q, k, v, g)
    ld_spec = whole(HEADS, TOK)
    map_specs = [per_head(DH, DH)] * 2
    mine, send, up0, con1, dec = call(
        k1_body, "k1",
        [smem()] + [seq()] * 4 + [ld_spec] + map_specs,
        [per_head(DH + 8, DH), per_head(DH + 8, DH),
         per_head(DH, DH), per_head(DH, DH), per_head(16, DH)],
        [shape((HEADS, DH + 8, DH)), shape((HEADS, DH + 8, DH)), MAT, MAT,
         shape((HEADS, 16, DH))],
        scratch=[pltpu.VMEM((HEADS, TOK), F32)],
    )(core, *seqs, ld, *maps)
    recv = swap_cores(send)
    packed = small(
        combine_body, "combine", 2, shape((CHIPS * (ROWS + 1), DH)), whole(CHIPS * (ROWS + 1), DH),
    )(pltpu.with_memory_space_constraint(mine, pltpu.HBM), recv)
    swapped = exchange(packed.reshape(CHIPS, (ROWS + 1) * DH), ("z", "x"))
    aq, bq, ak, bk, oi, vi, qd, kd, qt, kt, mark = call(
        k2_body, "k2",
        [smem()] + [seq()] * 4 + [ld_spec] + map_specs,
        [per_head(TOK, DH)] * 8 + [per_head(DH, TOK)] * 2 + [smem()],
        [HELD_B] * 4 + [HELD_F] * 2 + [HELD_B] * 2 + [shape((HEADS, DH, TOK), BF16)] * 2
        + [shape((1,), jnp.int32)],
        flops=1 << 30,
        after=1,
        scratch=[pltpu.VMEM((BLOCK, 3 * BLOCK), BF16), pltpu.VMEM((HEADS, TOK), F32)],
    )(packed, core, *seqs, ld, *maps)
    scanned = small(
        scan_body, "scan", 1, shape((CHIPS * ROWS, DH)), whole(CHIPS * ROWS, DH), smem=1,
    )(mark, swapped.reshape(CHIPS * (ROWS + 1), DH))
    inc = exchange(scanned.reshape(CHIPS, ROWS * DH), ("z", "x")).reshape(HEADS, DH, DH)
    passed = mine[:, DH:DH + 1, :] * inc + mine[:, :DH, :]
    recv = swap_cores(passed)
    st, af = small(
        states_body, "states", 5, [pltpu.HBM((HEADS, 2, DH, DH), BF16)] * 2,
        [whole(HEADS, 2, DH, DH)] * 2, smem=1,
    )(core, inc, recv, up0, con1, dec)
    gpq, gpk, mine, send = call(
        k3a_body, "k3a",
        [smem()] + [per_head(2, DH, DH)] * 2 + [per_head(DH, TOK)] * 2 + [seq()] * 2
        + [per_head(TOK, DH)] * 4,
        [per_head(TOK, DH)] * 2 + [per_head(DH, DH)] * 2,
        [HELD_B] * 2 + [MAT, MAT],
    )(core, st, af, qt, kt, v, g, aq, bq, ak, bk)
    recv = swap_cores(send)
    chip = small(add_body, "add", 2, MAT, whole(HEADS, DH, DH))(pltpu.with_memory_space_constraint(mine, pltpu.HBM), recv)
    pieces = exchange(chip.reshape(16, -1), ("x", "dp"))
    rows = HEADS * DH // 16
    out, gq, gk, gv, mark = call(
        k3b_body, "k3b",
        [smem()] + [per_head(TOK, DH)] * 4 + [per_head(2, DH, DH)] * 2 + [per_head(TOK, DH)] * 2 + map_specs,
        [seq()] * 4 + [smem()],
        [SEQ_B] * 4 + [shape((1,), jnp.int32)],
        flops=1 << 30,
        after=1,
    )(chip, core, oi, vi, qd, kd, st, af, gpq, gpk, *maps)
    spread = small(spread_first_body, "spread_z", 1, shape((8, rows, DH)), whole(8, rows, DH), smem=1)(
        mark, pieces.reshape(16, rows, DH)
    )
    pieces = exchange(spread.reshape(8, -1), "z")
    spread = small(spread_body, "spread_xy", 1, shape((16, rows, DH)), whole(16, rows, DH))(
        pieces.reshape(8, rows, DH)
    )
    own = exchange(spread.reshape(16, -1), ("x", "dp")).reshape(HEADS, DH, DH)
    other = swap_cores(own)
    first = core[0] == 0
    query_map_grad = jnp.where(first, own, other)
    key_map_grad = jnp.where(first, other, own)
    return (out[None], gq[None], gk[None], gv[None], query_map_grad, key_map_grad)


def solution(mesh):
    fine = Mesh(mesh.devices.reshape(8, 4, 2, 4), ("z", "x", "c", "dp"))
    ctx = ("z", "x", "c")
    act = P("dp", ctx, None)
    return jax.shard_map(
        local,
        mesh=fine,
        in_specs=(act, act, act, P("dp", None, ctx), act, P(), P()),
        out_specs=(act, act, act, act, P(), P()),
        check_vma=False,
    )
```

```python
import math

import jax
import jax.numpy as jnp
from jax import lax
from jax.experimental import pallas as pl
from jax.experimental.pallas import tpu as pltpu
from jax.sharding import Mesh, PartitionSpec as P

BLOCK = 256
HEADS = 8
DH = 128
TOK = 512
HPB = 2
WIDE = 4
SCALE = 1.0 / (DH * math.sqrt(BLOCK))
F32 = jnp.float32
BF16 = jnp.bfloat16
CHIPS = 32
ROWS = HEADS * DH // CHIPS


def dot(a, b, dims=((1,), (0,))):
    return lax.dot_general(a, b, (dims, ((), ())), preferred_element_type=F32)


NT = ((1,), (1,))
TN = ((0,), (0,))


def split3(x):
    hi = x.astype(BF16)
    rest = x - hi.astype(F32)
    mid = rest.astype(BF16)
    low = (rest - mid.astype(F32)).astype(BF16)
    return jnp.concatenate([hi, mid, low], axis=1)


def lower3():
    t = lax.broadcasted_iota(jnp.int32, (BLOCK, BLOCK), 0)
    s = lax.broadcasted_iota(jnp.int32, (BLOCK, BLOCK), 1)
    low = jnp.where(s <= t, 1.0, 0.0).astype(BF16)
    return jnp.concatenate([low, low, low], axis=1)


def cumul_cols(low, row):
    return dot(low, split3(jnp.broadcast_to(row, (DH, BLOCK))), NT)


def cumul_rows(low, rows):
    return dot(split3(rows), low, NT)


def sigmoid(u):
    return jax.nn.sigmoid(u)


def columns(ref, h):
    return ref.at[:, pl.ds(pl.multiple_of(h * DH, DH), DH)]


def head_copies(srcs, bufs, sems, h):
    return [
        pltpu.make_async_copy(columns(src, h) if len(src.shape) == 2 else src.at[h],
                              buf.at[h], sems.at[j, h])
        for j, (src, buf) in enumerate(zip(srcs, bufs))
    ]


def over_heads(srcs, bufs, sems, outs, out_sems, work):
    for h in range(HEADS):
        for copy in head_copies(srcs, bufs, sems, h):
            copy.start()

    def back(h):
        return [
            pltpu.make_async_copy(buf.at[h], dst.at[h], out_sems.at[j, h])
            for j, (buf, dst) in enumerate(outs)
        ]

    def some(step, carry):
        for i in range(HPB):
            for copy in head_copies(srcs, bufs, sems, step * HPB + i):
                copy.wait()
        for i in range(HPB):
            work(step * HPB + i)
        for i in range(HPB):
            for copy in back(step * HPB + i):
                copy.start()
        return carry

    lax.fori_loop(0, HEADS // HPB, some, 0)
    for h in range(HEADS):
        for copy in back(h):
            copy.wait()


def k1_body(core, ld_ref, q, k, v, g, wq, wk, mine_ref, send_ref, own,
            q_ref, k_ref, v_ref, g_ref, wq_ref, wk_ref, own_ref, cum_ref, sems, out_sems):
    first = core[0] == 0
    low = lower3()
    for b in range(2):
        rows = slice(b * BLOCK, (b + 1) * BLOCK)
        cum_ref[:, rows] = cumul_rows(low, ld_ref[:, rows])

    def work(h):
        ups, cons, tots = [], [], []
        all_q = dot(wq_ref[h], q_ref[h], ((0,), (1,)))
        all_k = dot(wk_ref[h], k_ref[h], ((0,), (1,)))
        for b in range(2):
            rows = slice(b * BLOCK, (b + 1) * BLOCK)
            cum = cum_ref[pl.ds(h, 1), rows]
            tot = cum[:, BLOCK - 1:BLOCK]
            pre_q = all_q[:, rows]
            pre_k = all_k[:, rows]
            qf = (pre_q * sigmoid(pre_q)).astype(BF16)
            kf = (pre_k * sigmoid(pre_k)).astype(BF16)
            qdec = (qf.astype(F32) * jnp.exp(cum)).astype(BF16)
            kdec = (kf.astype(F32) * jnp.exp(tot - cum)).astype(BF16)
            ups.append(dot(kdec, v_ref[h, rows]))
            cons.append(dot(qdec, g_ref[h, rows]))
            tots.append(jnp.broadcast_to(tot, (8, DH)))
        d0, d1 = jnp.exp(tots[0]), jnp.exp(tots[1])
        up = d1[0:1] * ups[0] + ups[1]
        con = cons[0] + d0[0:1] * cons[1]
        mine_ref[h, 0:DH, :] = jnp.where(first, up, con)
        send_ref[h, 0:DH, :] = jnp.where(first, con, up)
        mine_ref[h, DH:DH + 8, :] = d0 * d1
        send_ref[h, DH:DH + 8, :] = d0 * d1
        own_ref[h, 0:DH, :] = ups[0]
        own_ref[h, DH:2 * DH, :] = cons[1]
        own_ref[h, 2 * DH:2 * DH + 8, :] = d0
        own_ref[h, 2 * DH + 8:, :] = d1

    over_heads((q, k, v, g, wq, wk), (q_ref, k_ref, v_ref, g_ref, wq_ref, wk_ref), sems,
               [(own_ref, own)], out_sems, work)


def combine_body(mine_ref, recv_ref, out_ref):
    for h in range(HEADS):
        other = recv_ref[h, DH:DH + 1, :]
        agg = other * mine_ref[h, 0:DH, :] + recv_ref[h, 0:DH, :]
        both = other * mine_ref[h, DH:DH + 1, :]
        for part in range(DH // ROWS):
            at = (h * (DH // ROWS) + part) * (ROWS + 1)
            out_ref[at:at + ROWS, :] = agg[part * ROWS:(part + 1) * ROWS, :]
            out_ref[at + ROWS:at + ROWS + 1, :] = both


def scan_body(core, in_ref, out_ref):
    first = core[0] == 0

    def pieces(k):
        at = k * (ROWS + 1)
        return in_ref[at:at + ROWS, :], in_ref[at + ROWS:at + ROWS + 1, :]

    state = jnp.zeros((ROWS, DH), F32)
    for k in range(CHIPS):
        out_ref[k * ROWS:(k + 1) * ROWS, :] = state
        part, decay = pieces(k)
        state = decay * state + part
    state = jnp.zeros((ROWS, DH), F32)
    for k in range(CHIPS - 1, -1, -1):
        rows = slice(k * ROWS, (k + 1) * ROWS)
        out_ref[rows, :] = jnp.where(first, out_ref[rows, :], state)
        part, decay = pieces(k)
        state = decay * state + part


def k2_body(core, q_ref, k_ref, v_ref, g_ref, ld_ref, wq_ref, wk_ref,
            ab_ref, ov_ref, dec_ref, tr_ref, mark_ref, low_ref, cum_ref):
    step = pl.program_id(0)

    @pl.when(step == 0)
    def _():
        low_ref[...] = lower3()
        for b in range(2):
            rows = slice(b * BLOCK, (b + 1) * BLOCK)
            cum_ref[:, rows] = cumul_rows(low_ref[...], ld_ref[:, rows])

    t = lax.broadcasted_iota(jnp.int32, (BLOCK, BLOCK), 0)
    s = lax.broadcasted_iota(jnp.int32, (BLOCK, BLOCK), 1)
    causal = s <= t
    for i in range(HPB):
        lanes = slice(i * DH, (i + 1) * DH)
        tr_ref[i, 0] = q_ref[:, lanes].T
        tr_ref[i, 1] = k_ref[:, lanes].T
        for b in range(2):
            rows = slice(b * BLOCK, (b + 1) * BLOCK)
            head = pl.ds(step * HPB + i, 1)
            cum = cumul_cols(low_ref[...], ld_ref[head, rows])
            across = cum_ref[head, rows]
            tot = cum[BLOCK - 1:BLOCK, :]
            wide = jnp.concatenate([cum, cum], axis=1)
            weights = jnp.exp(jnp.where(causal, wide - across, -1e9))
            v, g = v_ref[rows, lanes], g_ref[rows, lanes]
            pre_q = dot(q_ref[rows, lanes], wq_ref[i])
            pre_k = dot(k_ref[rows, lanes], wk_ref[i])
            sig_q, sig_k = sigmoid(pre_q), sigmoid(pre_k)
            qf, kf = (pre_q * sig_q).astype(BF16), (pre_k * sig_k).astype(BF16)
            probs = (dot(qf, kf, NT) * weights).astype(BF16)
            grads = (dot(g, v, NT) * weights).astype(BF16)
            ov_ref[i, 0, rows] = SCALE * dot(probs, v)
            ov_ref[i, 1, rows] = SCALE * dot(probs, g, TN)
            early, late = jnp.exp(cum), jnp.exp(tot - cum)
            dec_ref[i, 0, rows] = (qf.astype(F32) * early).astype(BF16)
            dec_ref[i, 1, rows] = (kf.astype(F32) * late).astype(BF16)
            slope_q = SCALE * (sig_q * (1.0 + pre_q * (1.0 - sig_q)))
            ab_ref[i, 0, rows] = (dot(grads, kf) * slope_q).astype(BF16)
            ab_ref[i, 1, rows] = (early * slope_q).astype(BF16)
            slope_k = SCALE * (sig_k * (1.0 + pre_k * (1.0 - sig_k)))
            ab_ref[i, 2, rows] = (dot(grads, qf, TN) * slope_k).astype(BF16)
            ab_ref[i, 3, rows] = (late * slope_k).astype(BF16)
    mark_ref[0] = core[0]


def states_body(core, inc_ref, recv_ref, own_ref, st_ref):
    first = core[0] == 0
    for h in range(HEADS):
        inc, recv = inc_ref[h], recv_ref[h]
        state = jnp.where(first, inc, recv)
        after = jnp.where(first, recv, inc)
        d0, d1 = own_ref[h, 2 * DH:2 * DH + 1, :], own_ref[h, 2 * DH + 8:2 * DH + 9, :]
        st_ref[h, 0] = state.astype(BF16)
        st_ref[h, 1] = (d0 * state + own_ref[h, 0:DH, :]).astype(BF16)
        st_ref[h, 2] = (own_ref[h, DH:2 * DH, :] + d1 * after).astype(BF16)
        st_ref[h, 3] = after.astype(BF16)


def k3a_body(core, st, tr, v, g, ab, gp, mine_ref, send_ref,
             st_ref, tr_ref, v_ref, g_ref, ab_ref, gp_ref, sems, out_sems):
    first = core[0] == 0

    def work(h):
        for b in range(2):
            rows = slice(b * BLOCK, (b + 1) * BLOCK)
            from_state = dot(g_ref[h, rows], st_ref[h, b], NT)
            from_after = dot(v_ref[h, rows], st_ref[h, 2 + b], NT)
            gp_ref[h, 0, rows] = (
                ab_ref[h, 0, rows].astype(F32) + ab_ref[h, 1, rows].astype(F32) * from_state
            ).astype(BF16)
            gp_ref[h, 1, rows] = (
                ab_ref[h, 2, rows].astype(F32) + ab_ref[h, 3, rows].astype(F32) * from_after
            ).astype(BF16)
        part_q = dot(tr_ref[h, 0], gp_ref[h, 0])
        part_k = dot(tr_ref[h, 1], gp_ref[h, 1])
        mine_ref[h] = jnp.where(first, part_q, part_k)
        send_ref[h] = jnp.where(first, part_k, part_q)

    over_heads((st, tr, v, g, ab), (st_ref, tr_ref, v_ref, g_ref, ab_ref), sems,
               [(gp_ref, gp)], out_sems, work)


def k3b_body(core, ov_ref, dec_ref, st_ref, gp_ref, wq_ref, wk_ref,
             out_ref, gq_ref, gk_ref, gv_ref, mark_ref):
    mark_ref[0] = core[0]
    for i in range(WIDE):
        lanes = slice(i * DH, (i + 1) * DH)
        for b in range(2):
            rows = slice(b * BLOCK, (b + 1) * BLOCK)
            out_ref[rows, lanes] = (
                ov_ref[i, 0, rows] + SCALE * dot(dec_ref[i, 0, rows], st_ref[i, b])
            ).astype(BF16)
            gv_ref[rows, lanes] = (
                ov_ref[i, 1, rows] + SCALE * dot(dec_ref[i, 1, rows], st_ref[i, 2 + b])
            ).astype(BF16)
            gq_ref[rows, lanes] = dot(gp_ref[i, 0, rows], wq_ref[i], NT).astype(BF16)
            gk_ref[rows, lanes] = dot(gp_ref[i, 1, rows], wk_ref[i], NT).astype(BF16)


def add_body(a_ref, b_ref, out_ref):
    out_ref[...] = a_ref[...] + b_ref[...]


def spread_first_body(core, in_ref, out_ref):
    spread_body(in_ref, out_ref)


def spread_body(in_ref, out_ref):
    total = in_ref[0]
    for k in range(1, in_ref.shape[0]):
        total = total + in_ref[k]
    for k in range(out_ref.shape[0]):
        out_ref[k] = total


def smem():
    return pl.BlockSpec(memory_space=pltpu.SMEM)


def seq(heads=HPB):
    return pl.BlockSpec((TOK, heads * DH), lambda i: (0, i))


def per_head(*tail, heads=HPB):
    zeros = (0,) * len(tail)
    return pl.BlockSpec((heads,) + tail, lambda i: (i,) + zeros)


def whole(*shape):
    zeros = (0,) * len(shape)
    return pl.BlockSpec(shape, lambda i: zeros)


def shape(dims, kind=F32):
    return jax.ShapeDtypeStruct(dims, kind)


def call(body, name, ins, outs, out_shapes, flops=0, grid=HEADS // HPB, after=0,
         scratch=(), grant=None):
    return pl.pallas_call(
        lambda *refs: body(*refs[after:]),
        grid=(grid,),
        in_specs=[pl.BlockSpec(memory_space=pltpu.HBM)] * after + ins,
        out_specs=outs,
        out_shape=out_shapes,
        scratch_shapes=scratch,
        name=name,
        cost_estimate=pl.CostEstimate(flops=flops, transcendentals=0, bytes_accessed=1 << 20),
        compiler_params=pltpu.CompilerParams(
            dimension_semantics=("arbitrary",), vmem_limit_bytes=grant
        ),
    )


def streamed(body, name, slots, back, held, out_shapes, whole_ins=(), scratch=()):
    raw = pl.BlockSpec(memory_space=pltpu.HBM)
    kept = pl.BlockSpec(memory_space=pltpu.VMEM)
    return pl.pallas_call(
        body,
        grid=(1,),
        in_specs=[smem()] + list(whole_ins) + [raw] * len(slots),
        out_specs=[kept if here else raw for here in held],
        out_shape=out_shapes,
        scratch_shapes=list(slots) + list(back) + list(scratch) + [
            pltpu.SemaphoreType.DMA((len(slots), HEADS)),
            pltpu.SemaphoreType.DMA((len(back), HEADS)),
        ],
        name=name,
        compiler_params=pltpu.CompilerParams(dimension_semantics=("arbitrary",)),
    )


def small(body, name, ins, out_shape, out_spec, smem=0, after=0):
    vmem = pl.BlockSpec(memory_space=pltpu.VMEM)
    return pl.pallas_call(
        lambda *refs: body(*refs[after:]),
        grid=(1,),
        in_specs=[pl.BlockSpec(memory_space=pltpu.HBM)] * after
        + [pl.BlockSpec(memory_space=pltpu.SMEM)] * smem + [vmem] * ins,
        out_specs=out_spec,
        out_shape=out_shape,
        name=name,
        compiler_params=pltpu.CompilerParams(vmem_limit_bytes=8 << 20),
    )


def exchange(x, axes):
    return lax.all_to_all(x, axes, 0, 0, tiled=True)


def swap_cores(x):
    return lax.ppermute(x, "c", [(0, 1), (1, 0)])


SEQ_B = shape((TOK, HEADS * DH), BF16)
SEQ_F = shape((TOK, HEADS * DH), F32)
MAT = shape((HEADS, DH, DH), F32)


def local(query, key, value, log_decay, grad_out, query_map, key_map):
    core = lax.axis_index("c").astype(jnp.int32).reshape(1)
    q, k, v, g = (a[0] for a in (query, key, value, grad_out))
    ld = log_decay[0]
    maps = (query_map, key_map)
    seqs = (q, k, v, g)
    ld_spec = whole(HEADS, TOK)
    map_specs = [per_head(DH, DH)] * 2
    slot = pltpu.VMEM((HEADS, TOK, DH), BF16)
    square = pltpu.VMEM((HEADS, DH, DH), BF16)
    cut = pltpu.VMEM((HEADS, DH + 8, DH), F32)
    own_dims = (HEADS, 2 * DH + 16, DH)
    mine, send, own = streamed(
        k1_body, "k1", [slot] * 4 + [square] * 2, [pltpu.VMEM(own_dims, F32)],
        [True, True, False], [cut, cut, pltpu.HBM(own_dims, F32)],
        whole_ins=[ld_spec], scratch=[pltpu.VMEM((HEADS, TOK), F32)],
    )(core, ld, *seqs, *maps)
    recv = swap_cores(send)
    packed = small(
        combine_body, "combine", 2, shape((CHIPS * (ROWS + 1), DH)), whole(CHIPS * (ROWS + 1), DH),
    )(mine, recv)
    swapped = exchange(packed.reshape(CHIPS, (ROWS + 1) * DH), ("z", "x"))
    ab, ov, dec, tr, mark = call(
        k2_body, "k2",
        [smem()] + [seq()] * 4 + [ld_spec] + map_specs,
        [per_head(4, TOK, DH), per_head(2, TOK, DH), per_head(2, TOK, DH), per_head(2, DH, TOK),
         smem()],
        [shape((HEADS, 4, TOK, DH), BF16), shape((HEADS, 2, TOK, DH)),
         shape((HEADS, 2, TOK, DH), BF16), shape((HEADS, 2, DH, TOK), BF16),
         shape((1,), jnp.int32)],
        flops=1 << 30,
        after=1,
        scratch=[pltpu.VMEM((BLOCK, 3 * BLOCK), BF16), pltpu.VMEM((HEADS, TOK), F32)],
    )(packed, core, *seqs, ld, *maps)
    scanned = small(
        scan_body, "scan", 1, shape((CHIPS * ROWS, DH)), whole(CHIPS * ROWS, DH), smem=1,
    )(mark, swapped.reshape(CHIPS * (ROWS + 1), DH))
    inc = exchange(scanned.reshape(CHIPS, ROWS * DH), ("z", "x")).reshape(HEADS, DH, DH)
    passed = mine[:, DH:DH + 1, :] * inc + mine[:, :DH, :]
    recv = swap_cores(passed)
    st = small(
        states_body, "states", 3, pltpu.HBM((HEADS, 4, DH, DH), BF16), whole(HEADS, 4, DH, DH),
        smem=1,
    )(core, inc, recv, own)
    gp_dims = (HEADS, 2, TOK, DH)
    gp, mine, send = streamed(
        k3a_body, "k3a",
        [pltpu.VMEM((HEADS, 4, DH, DH), BF16), pltpu.VMEM((HEADS, 2, DH, TOK), BF16), slot, slot,
         pltpu.VMEM((HEADS, 4, TOK, DH), BF16)],
        [pltpu.VMEM(gp_dims, BF16)], [False, True, True],
        [pltpu.HBM(gp_dims, BF16), pltpu.VMEM((HEADS, DH, DH), F32),
         pltpu.VMEM((HEADS, DH, DH), F32)],
    )(core, st, tr, v, g, ab)
    recv = swap_cores(send)
    chip = small(add_body, "add", 2, MAT, whole(HEADS, DH, DH))(mine, recv)
    pieces = exchange(chip.reshape(16, -1), ("x", "dp"))
    rows = HEADS * DH // 16
    out, gq, gk, gv, mark = call(
        k3b_body, "k3b",
        [smem(), per_head(2, TOK, DH, heads=WIDE), per_head(2, TOK, DH, heads=WIDE),
         per_head(4, DH, DH, heads=WIDE), per_head(2, TOK, DH, heads=WIDE)]
        + [per_head(DH, DH, heads=WIDE)] * 2,
        [seq(WIDE)] * 4 + [smem()],

        [SEQ_B] * 4 + [shape((1,), jnp.int32)],
        flops=1 << 30,
        after=1,
        grid=HEADS // WIDE,
    )(chip, core, ov, dec, st, gp, *maps)
    spread = small(spread_first_body, "spread_z", 1, shape((8, rows, DH)), whole(8, rows, DH), smem=1)(
        mark, pieces.reshape(16, rows, DH)
    )
    pieces = exchange(spread.reshape(8, -1), "z")
    spread = small(spread_body, "spread_xy", 1, shape((16, rows, DH)), whole(16, rows, DH))(
        pieces.reshape(8, rows, DH)
    )
    own = exchange(spread.reshape(16, -1), ("x", "dp")).reshape(HEADS, DH, DH)
    other = swap_cores(own)
    first = core[0] == 0
    query_map_grad = jnp.where(first, own, other)
    key_map_grad = jnp.where(first, other, own)
    return (out[None], gq[None], gk[None], gv[None], query_map_grad, key_map_grad)


def solution(mesh):
    fine = Mesh(mesh.devices.reshape(8, 4, 2, 4), ("z", "x", "c", "dp"))
    ctx = ("z", "x", "c")
    act = P("dp", ctx, None)
    return jax.shard_map(
        local,
        mesh=fine,
        in_specs=(act, act, act, P("dp", None, ctx), act, P(), P()),
        out_specs=(act, act, act, act, P(), P()),
        check_vma=False,
    )
```

```python
import math

import jax
import jax.numpy as jnp
from jax import lax
from jax.experimental import pallas as pl
from jax.experimental.pallas import tpu as pltpu
from jax.sharding import Mesh, PartitionSpec as P

BLOCK = 256
HEADS = 8
DH = 128
TOK = 512
HPB = 2
WIDE = 4
SCALE = 1.0 / (DH * math.sqrt(BLOCK))
F32 = jnp.float32
BF16 = jnp.bfloat16
CHIPS = 32
ROWS = HEADS * DH // CHIPS


def dot(a, b, dims=((1,), (0,))):
    return lax.dot_general(a, b, (dims, ((), ())), preferred_element_type=F32)


NT = ((1,), (1,))
TN = ((0,), (0,))


def split3(x):
    hi = x.astype(BF16)
    rest = x - hi.astype(F32)
    mid = rest.astype(BF16)
    low = (rest - mid.astype(F32)).astype(BF16)
    return jnp.concatenate([hi, mid, low], axis=1)


def lower3():
    t = lax.broadcasted_iota(jnp.int32, (BLOCK, BLOCK), 0)
    s = lax.broadcasted_iota(jnp.int32, (BLOCK, BLOCK), 1)
    low = jnp.where(s <= t, 1.0, 0.0).astype(BF16)
    return jnp.concatenate([low, low, low], axis=1)


def cumul_cols(low, row):
    return dot(low, split3(jnp.broadcast_to(row, (DH, BLOCK))), NT)


def cumul_rows(low, rows):
    return dot(split3(rows), low, NT)


def sigmoid(u):
    return jax.nn.sigmoid(u)


def columns(ref, h):
    return ref.at[:, pl.ds(pl.multiple_of(h * DH, DH), DH)]


def head_copies(srcs, bufs, sems, h):
    return [
        pltpu.make_async_copy(columns(src, h) if len(src.shape) == 2 else src.at[h],
                              buf.at[h], sems.at[j, h])
        for j, (src, buf) in enumerate(zip(srcs, bufs))
    ]


def over_heads(srcs, bufs, sems, outs, out_sems, work):
    for h in range(HEADS):
        for copy in head_copies(srcs, bufs, sems, h):
            copy.start()

    def back(h):
        return [
            pltpu.make_async_copy(buf.at[h], dst.at[h], out_sems.at[j, h])
            for j, (buf, dst) in enumerate(outs)
        ]

    def some(step, carry):
        for i in range(HPB):
            for copy in head_copies(srcs, bufs, sems, step * HPB + i):
                copy.wait()
        for i in range(HPB):
            work(step * HPB + i)
        for i in range(HPB):
            for copy in back(step * HPB + i):
                copy.start()
        return carry

    lax.fori_loop(0, HEADS // HPB, some, 0)
    for h in range(HEADS):
        for copy in back(h):
            copy.wait()


def k1_body(core, ld_ref, q, k, v, g, wq, wk, mine_ref, send_ref, own,
            q_ref, k_ref, v_ref, g_ref, wq_ref, wk_ref, own_ref, cum_ref, sems, out_sems):
    first = core[0] == 0
    low = lower3()
    for b in range(2):
        rows = slice(b * BLOCK, (b + 1) * BLOCK)
        cum_ref[:, rows] = cumul_rows(low, ld_ref[:, rows])

    def work(h):
        ups, cons, tots = [], [], []
        all_q = dot(wq_ref[h], q_ref[h], ((0,), (1,)))
        all_k = dot(wk_ref[h], k_ref[h], ((0,), (1,)))
        for b in range(2):
            rows = slice(b * BLOCK, (b + 1) * BLOCK)
            cum = cum_ref[pl.ds(h, 1), rows]
            tot = cum[:, BLOCK - 1:BLOCK]
            pre_q = all_q[:, rows]
            pre_k = all_k[:, rows]
            qf = (pre_q * sigmoid(pre_q)).astype(BF16)
            kf = (pre_k * sigmoid(pre_k)).astype(BF16)
            qdec = (qf.astype(F32) * jnp.exp(cum)).astype(BF16)
            kdec = (kf.astype(F32) * jnp.exp(tot - cum)).astype(BF16)
            ups.append(dot(kdec, v_ref[h, rows]))
            cons.append(dot(qdec, g_ref[h, rows]))
            tots.append(jnp.broadcast_to(tot, (8, DH)))
        d0, d1 = jnp.exp(tots[0]), jnp.exp(tots[1])
        up = d1[0:1] * ups[0] + ups[1]
        con = cons[0] + d0[0:1] * cons[1]
        mine_ref[h, 0:DH, :] = jnp.where(first, up, con)
        send_ref[h, 0:DH, :] = jnp.where(first, con, up)
        mine_ref[h, DH:DH + 8, :] = d0 * d1
        send_ref[h, DH:DH + 8, :] = d0 * d1
        own_ref[h, 0:DH, :] = ups[0]
        own_ref[h, DH:2 * DH, :] = cons[1]
        own_ref[h, 2 * DH:2 * DH + 8, :] = d0
        own_ref[h, 2 * DH + 8:, :] = d1

    over_heads((q, k, v, g, wq, wk), (q_ref, k_ref, v_ref, g_ref, wq_ref, wk_ref), sems,
               [(own_ref, own)], out_sems, work)


def combine_body(mine_ref, recv_ref, out_ref):
    for h in range(HEADS):
        other = recv_ref[h, DH:DH + 1, :]
        agg = other * mine_ref[h, 0:DH, :] + recv_ref[h, 0:DH, :]
        both = other * mine_ref[h, DH:DH + 1, :]
        for part in range(DH // ROWS):
            at = (h * (DH // ROWS) + part) * (ROWS + 1)
            out_ref[at:at + ROWS, :] = agg[part * ROWS:(part + 1) * ROWS, :]
            out_ref[at + ROWS:at + ROWS + 1, :] = both


def scan_body(core, in_ref, out_ref):
    first = core[0] == 0

    def pieces(k):
        at = k * (ROWS + 1)
        return in_ref[at:at + ROWS, :], in_ref[at + ROWS:at + ROWS + 1, :]

    state = jnp.zeros((ROWS, DH), F32)
    for k in range(CHIPS):
        out_ref[k * ROWS:(k + 1) * ROWS, :] = state
        part, decay = pieces(k)
        state = decay * state + part
    state = jnp.zeros((ROWS, DH), F32)
    for k in range(CHIPS - 1, -1, -1):
        rows = slice(k * ROWS, (k + 1) * ROWS)
        out_ref[rows, :] = jnp.where(first, out_ref[rows, :], state)
        part, decay = pieces(k)
        state = decay * state + part


def k2_body(core, q_ref, k_ref, v_ref, g_ref, ld_ref, wq_ref, wk_ref,
            ab_ref, ov_ref, dec_ref, tr_ref, mark_ref, low_ref, cum_ref):
    step = pl.program_id(0)

    @pl.when(step == 0)
    def _():
        low_ref[...] = lower3()
        for b in range(2):
            rows = slice(b * BLOCK, (b + 1) * BLOCK)
            cum_ref[:, rows] = cumul_rows(low_ref[...], ld_ref[:, rows])

    t = lax.broadcasted_iota(jnp.int32, (BLOCK, BLOCK), 0)
    s = lax.broadcasted_iota(jnp.int32, (BLOCK, BLOCK), 1)
    causal = s <= t
    for i in range(HPB):
        lanes = slice(i * DH, (i + 1) * DH)
        tr_ref[i, 0] = q_ref[:, lanes].T
        tr_ref[i, 1] = k_ref[:, lanes].T
        for b in range(2):
            rows = slice(b * BLOCK, (b + 1) * BLOCK)
            head = pl.ds(step * HPB + i, 1)
            cum = cumul_cols(low_ref[...], ld_ref[head, rows])
            across = cum_ref[head, rows]
            tot = cum[BLOCK - 1:BLOCK, :]
            wide = jnp.concatenate([cum, cum], axis=1)
            weights = jnp.exp(jnp.where(causal, wide - across, -1e9))
            v, g = v_ref[rows, lanes], g_ref[rows, lanes]
            pre_q = dot(q_ref[rows, lanes], wq_ref[i])
            pre_k = dot(k_ref[rows, lanes], wk_ref[i])
            sig_q, sig_k = sigmoid(pre_q), sigmoid(pre_k)
            qf, kf = (pre_q * sig_q).astype(BF16), (pre_k * sig_k).astype(BF16)
            probs = (dot(qf, kf, NT) * weights).astype(BF16)
            grads = (dot(g, v, NT) * weights).astype(BF16)
            ov_ref[i, 0, rows] = SCALE * dot(probs, v)
            ov_ref[i, 1, rows] = SCALE * dot(probs, g, TN)
            early, late = jnp.exp(cum), jnp.exp(tot - cum)
            dec_ref[i, 0, rows] = (qf.astype(F32) * early).astype(BF16)
            dec_ref[i, 1, rows] = (kf.astype(F32) * late).astype(BF16)
            slope_q = SCALE * (sig_q * (1.0 + pre_q * (1.0 - sig_q)))
            ab_ref[i, 0, rows] = (dot(grads, kf) * slope_q).astype(BF16)
            ab_ref[i, 1, rows] = (early * slope_q).astype(BF16)
            slope_k = SCALE * (sig_k * (1.0 + pre_k * (1.0 - sig_k)))
            ab_ref[i, 2, rows] = (dot(grads, qf, TN) * slope_k).astype(BF16)
            ab_ref[i, 3, rows] = (late * slope_k).astype(BF16)
    mark_ref[0] = core[0]


def k3a_body(core, inc_ref, recv_ref, own_ref, v_ref, g_ref, tr, ab,
             gp, st, mine_ref, send_ref, tr_ref, ab_ref, gp_ref, st_ref, sems, out_sems):
    first = core[0] == 0

    def work(h):
        lanes = pl.ds(pl.multiple_of(h * DH, DH), DH)
        inc, recv = inc_ref[h], recv_ref[h]
        state = jnp.where(first, inc, recv)
        after = jnp.where(first, recv, inc)
        d0, d1 = own_ref[h, 2 * DH:2 * DH + 1, :], own_ref[h, 2 * DH + 8:2 * DH + 9, :]
        st_ref[h, 0] = state.astype(BF16)
        st_ref[h, 1] = (d0 * state + own_ref[h, 0:DH, :]).astype(BF16)
        st_ref[h, 2] = (own_ref[h, DH:2 * DH, :] + d1 * after).astype(BF16)
        st_ref[h, 3] = after.astype(BF16)
        for b in range(2):
            rows = slice(b * BLOCK, (b + 1) * BLOCK)
            from_state = dot(g_ref[rows, lanes], st_ref[h, b], NT)
            from_after = dot(v_ref[rows, lanes], st_ref[h, 2 + b], NT)
            gp_ref[h, 0, rows] = (
                ab_ref[h, 0, rows].astype(F32) + ab_ref[h, 1, rows].astype(F32) * from_state
            ).astype(BF16)
            gp_ref[h, 1, rows] = (
                ab_ref[h, 2, rows].astype(F32) + ab_ref[h, 3, rows].astype(F32) * from_after
            ).astype(BF16)
        part_q = dot(tr_ref[h, 0], gp_ref[h, 0])
        part_k = dot(tr_ref[h, 1], gp_ref[h, 1])
        mine_ref[h] = jnp.where(first, part_q, part_k)
        send_ref[h] = jnp.where(first, part_k, part_q)

    over_heads((tr, ab), (tr_ref, ab_ref), sems,
               [(gp_ref, gp), (st_ref, st)], out_sems, work)


def k3b_body(core, ov_ref, dec_ref, st_ref, gp_ref, wq_ref, wk_ref,
             out_ref, gq_ref, gk_ref, gv_ref, mark_ref):
    mark_ref[0] = core[0]
    for i in range(WIDE):
        lanes = slice(i * DH, (i + 1) * DH)
        for b in range(2):
            rows = slice(b * BLOCK, (b + 1) * BLOCK)
            out_ref[rows, lanes] = (
                ov_ref[i, 0, rows] + SCALE * dot(dec_ref[i, 0, rows], st_ref[i, b])
            ).astype(BF16)
            gv_ref[rows, lanes] = (
                ov_ref[i, 1, rows] + SCALE * dot(dec_ref[i, 1, rows], st_ref[i, 2 + b])
            ).astype(BF16)
            gq_ref[rows, lanes] = dot(gp_ref[i, 0, rows], wq_ref[i], NT).astype(BF16)
            gk_ref[rows, lanes] = dot(gp_ref[i, 1, rows], wk_ref[i], NT).astype(BF16)


def add_body(a_ref, b_ref, out_ref):
    out_ref[...] = a_ref[...] + b_ref[...]


def pass_body(mine_ref, inc_ref, out_ref):
    for h in range(HEADS):
        out_ref[h] = mine_ref[h, DH:DH + 1, :] * inc_ref[h] + mine_ref[h, 0:DH, :]


def spread_first_body(core, in_ref, out_ref):
    spread_body(in_ref, out_ref)


def spread_body(in_ref, out_ref):
    total = in_ref[0]
    for k in range(1, in_ref.shape[0]):
        total = total + in_ref[k]
    for k in range(out_ref.shape[0]):
        out_ref[k] = total


def smem():
    return pl.BlockSpec(memory_space=pltpu.SMEM)


def seq(heads=HPB):
    return pl.BlockSpec((TOK, heads * DH), lambda i: (0, i))


def per_head(*tail, heads=HPB):
    zeros = (0,) * len(tail)
    return pl.BlockSpec((heads,) + tail, lambda i: (i,) + zeros)


def whole(*shape):
    zeros = (0,) * len(shape)
    return pl.BlockSpec(shape, lambda i: zeros)


def shape(dims, kind=F32):
    return jax.ShapeDtypeStruct(dims, kind)


def call(body, name, ins, outs, out_shapes, flops=0, grid=HEADS // HPB, after=0,
         scratch=(), grant=None):
    return pl.pallas_call(
        lambda *refs: body(*refs[after:]),
        grid=(grid,),
        in_specs=[pl.BlockSpec(memory_space=pltpu.HBM)] * after + ins,
        out_specs=outs,
        out_shape=out_shapes,
        scratch_shapes=scratch,
        name=name,
        cost_estimate=pl.CostEstimate(flops=flops, transcendentals=0, bytes_accessed=1 << 20),
        compiler_params=pltpu.CompilerParams(
            dimension_semantics=("arbitrary",), vmem_limit_bytes=grant
        ),
    )


def streamed(body, name, slots, back, held, out_shapes, whole_ins=(), scratch=(),
             grant=None):
    raw = pl.BlockSpec(memory_space=pltpu.HBM)
    kept = pl.BlockSpec(memory_space=pltpu.VMEM)
    return pl.pallas_call(
        body,
        grid=(1,),
        in_specs=[smem()] + list(whole_ins) + [raw] * len(slots),
        out_specs=[kept if here else raw for here in held],
        out_shape=out_shapes,
        scratch_shapes=list(slots) + list(back) + list(scratch) + [
            pltpu.SemaphoreType.DMA((len(slots), HEADS)),
            pltpu.SemaphoreType.DMA((len(back), HEADS)),
        ],
        name=name,
        compiler_params=pltpu.CompilerParams(
            dimension_semantics=("arbitrary",), vmem_limit_bytes=grant
        ),
    )


def small(body, name, ins, out_shape, out_spec, smem=0, after=0):
    vmem = pl.BlockSpec(memory_space=pltpu.VMEM)
    return pl.pallas_call(
        lambda *refs: body(*refs[after:]),
        grid=(1,),
        in_specs=[pl.BlockSpec(memory_space=pltpu.HBM)] * after
        + [pl.BlockSpec(memory_space=pltpu.SMEM)] * smem + [vmem] * ins,
        out_specs=out_spec,
        out_shape=out_shape,
        name=name,
        compiler_params=pltpu.CompilerParams(vmem_limit_bytes=8 << 20),
    )


def exchange(x, axes):
    return lax.all_to_all(x, axes, 0, 0, tiled=True)


def swap_cores(x):
    return lax.ppermute(x, "c", [(0, 1), (1, 0)])


SEQ_B = shape((TOK, HEADS * DH), BF16)
SEQ_F = shape((TOK, HEADS * DH), F32)
MAT = shape((HEADS, DH, DH), F32)


def local(query, key, value, log_decay, grad_out, query_map, key_map):
    core = lax.axis_index("c").astype(jnp.int32).reshape(1)
    q, k, v, g = (a[0] for a in (query, key, value, grad_out))
    ld = log_decay[0]
    maps = (query_map, key_map)
    seqs = (q, k, v, g)
    ld_spec = whole(HEADS, TOK)
    map_specs = [per_head(DH, DH)] * 2
    slot = pltpu.VMEM((HEADS, TOK, DH), BF16)
    square = pltpu.VMEM((HEADS, DH, DH), BF16)
    cut = pltpu.VMEM((HEADS, DH + 8, DH), F32)
    own_dims = (HEADS, 2 * DH + 16, DH)
    mine, send, own = streamed(
        k1_body, "k1", [slot] * 4 + [square] * 2, [pltpu.VMEM(own_dims, F32)],
        [True, True, False], [cut, cut, pltpu.HBM(own_dims, F32)],
        whole_ins=[ld_spec], scratch=[pltpu.VMEM((HEADS, TOK), F32)],
    )(core, ld, *seqs, *maps)
    recv = swap_cores(send)
    packed = small(
        combine_body, "combine", 2, shape((CHIPS * (ROWS + 1), DH)), whole(CHIPS * (ROWS + 1), DH),
    )(mine, recv)
    swapped = exchange(packed.reshape(CHIPS, (ROWS + 1) * DH), ("z", "x"))
    ab, ov, dec, tr, mark = call(
        k2_body, "k2",
        [smem()] + [seq()] * 4 + [ld_spec] + map_specs,
        [per_head(4, TOK, DH), per_head(2, TOK, DH), per_head(2, TOK, DH), per_head(2, DH, TOK),
         smem()],
        [shape((HEADS, 4, TOK, DH), BF16), shape((HEADS, 2, TOK, DH)),
         shape((HEADS, 2, TOK, DH), BF16), shape((HEADS, 2, DH, TOK), BF16),
         shape((1,), jnp.int32)],
        flops=1 << 30,
        after=1,
        scratch=[pltpu.VMEM((BLOCK, 3 * BLOCK), BF16), pltpu.VMEM((HEADS, TOK), F32)],
    )(packed, core, *seqs, ld, *maps)
    scanned = small(
        scan_body, "scan", 1, pltpu.VMEM((CHIPS * ROWS, DH), F32),
        pl.BlockSpec(memory_space=pltpu.VMEM), smem=1,
    )(mark, swapped.reshape(CHIPS * (ROWS + 1), DH))
    inc = exchange(scanned.reshape(CHIPS, ROWS * DH), ("z", "x")).reshape(HEADS, DH, DH)
    passed = small(
        pass_body, "pass", 2, pltpu.VMEM((HEADS, DH, DH), F32),
        pl.BlockSpec(memory_space=pltpu.VMEM),
    )(mine, inc)
    recv = swap_cores(passed)
    gp_dims = (HEADS, 2, TOK, DH)
    st_dims = (HEADS, 4, DH, DH)
    half = pltpu.VMEM((HEADS, DH, DH), F32)
    gp, st, mine, send = streamed(
        k3a_body, "k3a",
        [pltpu.VMEM((HEADS, 2, DH, TOK), BF16), pltpu.VMEM((HEADS, 4, TOK, DH), BF16)],
        [pltpu.VMEM(gp_dims, BF16), pltpu.VMEM(st_dims, BF16)], [False, False, True, True],
        [pltpu.HBM(gp_dims, BF16), pltpu.HBM(st_dims, BF16), half, half],
        whole_ins=[pl.BlockSpec(memory_space=pltpu.VMEM)] * 5, grant=20 << 20,
    )(core, inc, recv, own, v, g,
      *(pltpu.with_memory_space_constraint(x, pltpu.HBM) for x in (tr, ab)))
    recv = swap_cores(send)
    chip = small(add_body, "add", 2, MAT, whole(HEADS, DH, DH))(mine, recv)
    pieces = exchange(chip.reshape(16, -1), ("x", "dp"))
    rows = HEADS * DH // 16
    out, gq, gk, gv, mark = call(
        k3b_body, "k3b",
        [smem(), per_head(2, TOK, DH, heads=WIDE), per_head(2, TOK, DH, heads=WIDE),
         per_head(4, DH, DH, heads=WIDE), per_head(2, TOK, DH, heads=WIDE)]
        + [per_head(DH, DH, heads=WIDE)] * 2,
        [seq(WIDE)] * 4 + [smem()],

        [SEQ_B] * 4 + [shape((1,), jnp.int32)],
        flops=1 << 30,
        after=1,
        grid=HEADS // WIDE,
    )(chip, core, ov, dec, st, gp, *maps)
    spread = small(spread_first_body, "spread_z", 1, shape((8, rows, DH)), whole(8, rows, DH), smem=1)(
        mark, pieces.reshape(16, rows, DH)
    )
    pieces = exchange(spread.reshape(8, -1), "z")
    spread = small(spread_body, "spread_xy", 1, shape((16, rows, DH)), whole(16, rows, DH))(
        pieces.reshape(8, rows, DH)
    )
    own = exchange(spread.reshape(16, -1), ("x", "dp")).reshape(HEADS, DH, DH)
    other = swap_cores(own)
    first = core[0] == 0
    query_map_grad = jnp.where(first, own, other)
    key_map_grad = jnp.where(first, other, own)
    return (out[None], gq[None], gk[None], gv[None], query_map_grad, key_map_grad)


def solution(mesh):
    fine = Mesh(mesh.devices.reshape(8, 4, 2, 4), ("z", "x", "c", "dp"))
    ctx = ("z", "x", "c")
    act = P("dp", ctx, None)
    return jax.shard_map(
        local,
        mesh=fine,
        in_specs=(act, act, act, P("dp", None, ctx), act, P(), P()),
        out_specs=(act, act, act, act, P(), P()),
        check_vma=False,
    )
```

```python
import math

import jax
import jax.numpy as jnp
from jax import lax
from jax.experimental import pallas as pl
from jax.experimental.pallas import tpu as pltpu
from jax.sharding import Mesh, PartitionSpec as P

BLOCK = 256
HEADS = 8
DH = 128
TOK = 512
HPB = 2
WIDE = 4
SCALE = 1.0 / (DH * math.sqrt(BLOCK))
F32 = jnp.float32
BF16 = jnp.bfloat16
CHIPS = 32
ROWS = HEADS * DH // CHIPS


def dot(a, b, dims=((1,), (0,))):
    return lax.dot_general(a, b, (dims, ((), ())), preferred_element_type=F32)


NT = ((1,), (1,))
TN = ((0,), (0,))


def split3(x):
    hi = x.astype(BF16)
    rest = x - hi.astype(F32)
    mid = rest.astype(BF16)
    low = (rest - mid.astype(F32)).astype(BF16)
    return jnp.concatenate([hi, mid, low], axis=1)


def lower3():
    t = lax.broadcasted_iota(jnp.int32, (BLOCK, BLOCK), 0)
    s = lax.broadcasted_iota(jnp.int32, (BLOCK, BLOCK), 1)
    low = jnp.where(s <= t, 1.0, 0.0).astype(BF16)
    return jnp.concatenate([low, low, low], axis=1)


def cumul_cols(low, row):
    return dot(low, split3(jnp.broadcast_to(row, (DH, BLOCK))), NT)


def cumul_rows(low, rows):
    return dot(split3(rows), low, NT)


def sigmoid(u):
    return jax.nn.sigmoid(u)


def columns(ref, h):
    return ref.at[:, pl.ds(pl.multiple_of(h * DH, DH), DH)]


def head_copies(srcs, bufs, sems, h):
    return [
        pltpu.make_async_copy(columns(src, h) if len(src.shape) == 2 else src.at[h],
                              buf.at[h], sems.at[j, h])
        for j, (src, buf) in enumerate(zip(srcs, bufs))
    ]


def over_heads(srcs, bufs, sems, outs, out_sems, work, before=None):
    for h in range(HEADS):
        for copy in head_copies(srcs, bufs, sems, h):
            copy.start()
    if before is not None:
        before()

    def back(h):
        return [
            pltpu.make_async_copy(buf.at[h], dst.at[h], out_sems.at[j, h])
            for j, (buf, dst) in enumerate(outs)
        ]

    def some(step, carry):
        for i in range(HPB):
            for copy in head_copies(srcs, bufs, sems, step * HPB + i):
                copy.wait()
        for i in range(HPB):
            work(step * HPB + i)
        for i in range(HPB):
            for copy in back(step * HPB + i):
                copy.start()
        return carry

    lax.fori_loop(0, HEADS // HPB, some, 0)
    for h in range(HEADS):
        for copy in back(h):
            copy.wait()


def k1_body(core, ld, q, k, v, g, wq, wk, mine_ref, send_ref, own,
            q_ref, k_ref, v_ref, g_ref, wq_ref, wk_ref, own_ref, ld_ref, cum_ref, ld_sem,
            sems, out_sems):
    first = core[0] == 0
    decays = pltpu.make_async_copy(ld, ld_ref, ld_sem.at[0])
    decays.start()

    def running_sums():
        low = lower3()
        decays.wait()
        for b in range(2):
            rows = slice(b * BLOCK, (b + 1) * BLOCK)
            cum_ref[:, rows] = cumul_rows(low, ld_ref[:, rows])

    def work(h):
        ups, cons, tots = [], [], []
        all_q = dot(wq_ref[h], q_ref[h], ((0,), (1,)))
        all_k = dot(wk_ref[h], k_ref[h], ((0,), (1,)))
        for b in range(2):
            rows = slice(b * BLOCK, (b + 1) * BLOCK)
            cum = cum_ref[pl.ds(h, 1), rows]
            tot = cum[:, BLOCK - 1:BLOCK]
            pre_q = all_q[:, rows]
            pre_k = all_k[:, rows]
            qf = (pre_q * sigmoid(pre_q)).astype(BF16)
            kf = (pre_k * sigmoid(pre_k)).astype(BF16)
            qdec = (qf.astype(F32) * jnp.exp(cum)).astype(BF16)
            kdec = (kf.astype(F32) * jnp.exp(tot - cum)).astype(BF16)
            ups.append(dot(kdec, v_ref[h, rows]))
            cons.append(dot(qdec, g_ref[h, rows]))
            tots.append(jnp.broadcast_to(tot, (8, DH)))
        d0, d1 = jnp.exp(tots[0]), jnp.exp(tots[1])
        up = d1[0:1] * ups[0] + ups[1]
        con = cons[0] + d0[0:1] * cons[1]
        mine_ref[h, 0:DH, :] = jnp.where(first, up, con)
        send_ref[h, 0:DH, :] = jnp.where(first, con, up)
        mine_ref[h, DH:DH + 8, :] = d0 * d1
        send_ref[h, DH:DH + 8, :] = d0 * d1
        own_ref[h, 0:DH, :] = ups[0]
        own_ref[h, DH:2 * DH, :] = cons[1]
        own_ref[h, 2 * DH:2 * DH + 8, :] = d0
        own_ref[h, 2 * DH + 8:, :] = d1

    over_heads((q, k, v, g, wq, wk), (q_ref, k_ref, v_ref, g_ref, wq_ref, wk_ref), sems,
               [(own_ref, own)], out_sems, work, running_sums)


def combine_body(mine_ref, recv_ref, out_ref):
    for h in range(HEADS):
        other = recv_ref[h, DH:DH + 1, :]
        agg = other * mine_ref[h, 0:DH, :] + recv_ref[h, 0:DH, :]
        both = other * mine_ref[h, DH:DH + 1, :]
        for part in range(DH // ROWS):
            at = (h * (DH // ROWS) + part) * (ROWS + 1)
            out_ref[at:at + ROWS, :] = agg[part * ROWS:(part + 1) * ROWS, :]
            out_ref[at + ROWS:at + ROWS + 1, :] = both


def scan_body(core, in_ref, out_ref):
    first = core[0] == 0

    def pieces(k):
        at = k * (ROWS + 1)
        return in_ref[at:at + ROWS, :], in_ref[at + ROWS:at + ROWS + 1, :]

    state = jnp.zeros((ROWS, DH), F32)
    for k in range(CHIPS):
        out_ref[k * ROWS:(k + 1) * ROWS, :] = state
        part, decay = pieces(k)
        state = decay * state + part
    state = jnp.zeros((ROWS, DH), F32)
    for k in range(CHIPS - 1, -1, -1):
        rows = slice(k * ROWS, (k + 1) * ROWS)
        out_ref[rows, :] = jnp.where(first, out_ref[rows, :], state)
        part, decay = pieces(k)
        state = decay * state + part


def k2_body(core, q_ref, k_ref, v_ref, g_ref, ld_ref, wq_ref, wk_ref,
            ab_ref, ov_ref, dec_ref, tr_ref, mark_ref, low_ref, cum_ref):
    step = pl.program_id(0)

    @pl.when(step == 0)
    def _():
        low_ref[...] = lower3()
        for b in range(2):
            rows = slice(b * BLOCK, (b + 1) * BLOCK)
            cum_ref[:, rows] = cumul_rows(low_ref[...], ld_ref[:, rows])

    t = lax.broadcasted_iota(jnp.int32, (BLOCK, BLOCK), 0)
    s = lax.broadcasted_iota(jnp.int32, (BLOCK, BLOCK), 1)
    causal = s <= t
    for i in range(HPB):
        lanes = slice(i * DH, (i + 1) * DH)
        tr_ref[i, 0] = q_ref[:, lanes].T
        tr_ref[i, 1] = k_ref[:, lanes].T
        for b in range(2):
            rows = slice(b * BLOCK, (b + 1) * BLOCK)
            head = pl.ds(step * HPB + i, 1)
            cum = cumul_cols(low_ref[...], ld_ref[head, rows])
            across = cum_ref[head, rows]
            tot = cum[BLOCK - 1:BLOCK, :]
            wide = jnp.concatenate([cum, cum], axis=1)
            weights = jnp.exp(jnp.where(causal, wide - across, -1e9))
            v, g = v_ref[rows, lanes], g_ref[rows, lanes]
            pre_q = dot(q_ref[rows, lanes], wq_ref[i])
            pre_k = dot(k_ref[rows, lanes], wk_ref[i])
            sig_q, sig_k = sigmoid(pre_q), sigmoid(pre_k)
            qf, kf = (pre_q * sig_q).astype(BF16), (pre_k * sig_k).astype(BF16)
            probs = (dot(qf, kf, NT) * weights).astype(BF16)
            grads = (dot(g, v, NT) * weights).astype(BF16)
            ov_ref[i, 0, rows] = SCALE * dot(probs, v)
            ov_ref[i, 1, rows] = SCALE * dot(probs, g, TN)
            early, late = jnp.exp(cum), jnp.exp(tot - cum)
            dec_ref[i, 0, rows] = (qf.astype(F32) * early).astype(BF16)
            dec_ref[i, 1, rows] = (kf.astype(F32) * late).astype(BF16)
            slope_q = SCALE * (sig_q * (1.0 + pre_q * (1.0 - sig_q)))
            ab_ref[i, 0, rows] = (dot(grads, kf) * slope_q).astype(BF16)
            ab_ref[i, 1, rows] = (early * slope_q).astype(BF16)
            slope_k = SCALE * (sig_k * (1.0 + pre_k * (1.0 - sig_k)))
            ab_ref[i, 2, rows] = (dot(grads, qf, TN) * slope_k).astype(BF16)
            ab_ref[i, 3, rows] = (late * slope_k).astype(BF16)
    mark_ref[0] = core[0]


def k3a_body(core, inc_ref, recv_ref, own_ref, v_ref, g_ref, tr, ab,
             gp, st, mine_ref, send_ref, tr_ref, ab_ref, gp_ref, st_ref, sems, out_sems):
    first = core[0] == 0

    def work(h):
        lanes = pl.ds(pl.multiple_of(h * DH, DH), DH)
        inc, recv = inc_ref[h], recv_ref[h]
        state = jnp.where(first, inc, recv)
        after = jnp.where(first, recv, inc)
        d0, d1 = own_ref[h, 2 * DH:2 * DH + 1, :], own_ref[h, 2 * DH + 8:2 * DH + 9, :]
        st_ref[h, 0] = state.astype(BF16)
        st_ref[h, 1] = (d0 * state + own_ref[h, 0:DH, :]).astype(BF16)
        st_ref[h, 2] = (own_ref[h, DH:2 * DH, :] + d1 * after).astype(BF16)
        st_ref[h, 3] = after.astype(BF16)
        for b in range(2):
            rows = slice(b * BLOCK, (b + 1) * BLOCK)
            from_state = dot(g_ref[rows, lanes], st_ref[h, b], NT)
            from_after = dot(v_ref[rows, lanes], st_ref[h, 2 + b], NT)
            gp_ref[h, 0, rows] = (
                ab_ref[h, 0, rows].astype(F32) + ab_ref[h, 1, rows].astype(F32) * from_state
            ).astype(BF16)
            gp_ref[h, 1, rows] = (
                ab_ref[h, 2, rows].astype(F32) + ab_ref[h, 3, rows].astype(F32) * from_after
            ).astype(BF16)
        part_q = dot(tr_ref[h, 0], gp_ref[h, 0])
        part_k = dot(tr_ref[h, 1], gp_ref[h, 1])
        mine_ref[h] = jnp.where(first, part_q, part_k)
        send_ref[h] = jnp.where(first, part_k, part_q)

    over_heads((tr, ab), (tr_ref, ab_ref), sems,
               [(gp_ref, gp), (st_ref, st)], out_sems, work)


def k3b_body(core, ov_ref, dec_ref, st_ref, out_ref, gv_ref, mark_ref):
    mark_ref[0] = core[0]
    for i in range(WIDE):
        lanes = slice(i * DH, (i + 1) * DH)
        for b in range(2):
            rows = slice(b * BLOCK, (b + 1) * BLOCK)
            out_ref[rows, lanes] = (
                ov_ref[i, 0, rows] + SCALE * dot(dec_ref[i, 0, rows], st_ref[i, b])
            ).astype(BF16)
            gv_ref[rows, lanes] = (
                ov_ref[i, 1, rows] + SCALE * dot(dec_ref[i, 1, rows], st_ref[i, 2 + b])
            ).astype(BF16)


def k3c_body(core, gp_ref, wq_ref, wk_ref, gq_ref, gk_ref, mark_ref):
    mark_ref[0] = core[0]
    for i in range(WIDE):
        lanes = slice(i * DH, (i + 1) * DH)
        gq_ref[:, lanes] = dot(gp_ref[i, 0], wq_ref[i], NT).astype(BF16)
        gk_ref[:, lanes] = dot(gp_ref[i, 1], wk_ref[i], NT).astype(BF16)


def add_body(a_ref, b_ref, out_ref):
    out_ref[...] = a_ref[...] + b_ref[...]


def pass_body(mine_ref, inc_ref, out_ref):
    for h in range(HEADS):
        out_ref[h] = mine_ref[h, DH:DH + 1, :] * inc_ref[h] + mine_ref[h, 0:DH, :]


def spread_first_body(core, in_ref, out_ref):
    spread_body(in_ref, out_ref)


def spread_body(in_ref, out_ref):
    total = in_ref[0]
    for k in range(1, in_ref.shape[0]):
        total = total + in_ref[k]
    for k in range(out_ref.shape[0]):
        out_ref[k] = total


def smem():
    return pl.BlockSpec(memory_space=pltpu.SMEM)


def seq(heads=HPB):
    return pl.BlockSpec((TOK, heads * DH), lambda i: (0, i))


def per_head(*tail, heads=HPB):
    zeros = (0,) * len(tail)
    return pl.BlockSpec((heads,) + tail, lambda i: (i,) + zeros)


def whole(*shape):
    zeros = (0,) * len(shape)
    return pl.BlockSpec(shape, lambda i: zeros)


def shape(dims, kind=F32):
    return jax.ShapeDtypeStruct(dims, kind)


def call(body, name, ins, outs, out_shapes, flops=0, grid=HEADS // HPB, after=0,
         scratch=(), grant=None):
    return pl.pallas_call(
        lambda *refs: body(*refs[after:]),
        grid=(grid,),
        in_specs=[pl.BlockSpec(memory_space=pltpu.HBM)] * after + ins,
        out_specs=outs,
        out_shape=out_shapes,
        scratch_shapes=scratch,
        name=name,
        cost_estimate=pl.CostEstimate(flops=flops, transcendentals=0, bytes_accessed=1 << 20),
        compiler_params=pltpu.CompilerParams(
            dimension_semantics=("arbitrary",), vmem_limit_bytes=grant
        ),
    )


def streamed(body, name, slots, back, held, out_shapes, whole_ins=(), scratch=(),
             grant=None):
    raw = pl.BlockSpec(memory_space=pltpu.HBM)
    kept = pl.BlockSpec(memory_space=pltpu.VMEM)
    return pl.pallas_call(
        body,
        grid=(1,),
        in_specs=[smem()] + list(whole_ins) + [raw] * len(slots),
        out_specs=[kept if here else raw for here in held],
        out_shape=out_shapes,
        scratch_shapes=list(slots) + list(back) + list(scratch) + [
            pltpu.SemaphoreType.DMA((len(slots), HEADS)),
            pltpu.SemaphoreType.DMA((len(back), HEADS)),
        ],
        name=name,
        compiler_params=pltpu.CompilerParams(
            dimension_semantics=("arbitrary",), vmem_limit_bytes=grant
        ),
    )


def small(body, name, ins, out_shape, out_spec, smem=0, after=0):
    vmem = pl.BlockSpec(memory_space=pltpu.VMEM)
    return pl.pallas_call(
        lambda *refs: body(*refs[after:]),
        grid=(1,),
        in_specs=[pl.BlockSpec(memory_space=pltpu.HBM)] * after
        + [pl.BlockSpec(memory_space=pltpu.SMEM)] * smem + [vmem] * ins,
        out_specs=out_spec,
        out_shape=out_shape,
        name=name,
        compiler_params=pltpu.CompilerParams(vmem_limit_bytes=8 << 20),
    )


def exchange(x, axes):
    return lax.all_to_all(x, axes, 0, 0, tiled=True)


def swap_cores(x):
    return lax.ppermute(x, "c", [(0, 1), (1, 0)])


SEQ_B = shape((TOK, HEADS * DH), BF16)
SEQ_F = shape((TOK, HEADS * DH), F32)
MAT = shape((HEADS, DH, DH), F32)


def local(query, key, value, log_decay, grad_out, query_map, key_map):
    core = lax.axis_index("c").astype(jnp.int32).reshape(1)
    q, k, v, g = (a[0] for a in (query, key, value, grad_out))
    ld = log_decay[0]
    maps = (query_map, key_map)
    seqs = (q, k, v, g)
    ld_spec = whole(HEADS, TOK)
    map_specs = [per_head(DH, DH)] * 2
    slot = pltpu.VMEM((HEADS, TOK, DH), BF16)
    square = pltpu.VMEM((HEADS, DH, DH), BF16)
    cut = pltpu.VMEM((HEADS, DH + 8, DH), F32)
    own_dims = (HEADS, 2 * DH + 16, DH)
    mine, send, own = streamed(
        k1_body, "k1", [slot] * 4 + [square] * 2, [pltpu.VMEM(own_dims, F32)],
        [True, True, False], [cut, cut, pltpu.HBM(own_dims, F32)],
        whole_ins=[pl.BlockSpec(memory_space=pltpu.HBM)],
        scratch=[pltpu.VMEM((HEADS, TOK), F32)] * 2 + [pltpu.SemaphoreType.DMA((1,))],
    )(core, ld, *seqs, *maps)
    recv = swap_cores(send)
    packed = small(
        combine_body, "combine", 2, shape((CHIPS * (ROWS + 1), DH)), whole(CHIPS * (ROWS + 1), DH),
    )(mine, recv)
    swapped = exchange(packed.reshape(CHIPS, (ROWS + 1) * DH), ("z", "x"))
    ab, ov, dec, tr, mark = call(
        k2_body, "k2",
        [smem()] + [seq()] * 4 + [ld_spec] + map_specs,
        [per_head(4, TOK, DH), per_head(2, TOK, DH), per_head(2, TOK, DH), per_head(2, DH, TOK),
         smem()],
        [shape((HEADS, 4, TOK, DH), BF16), shape((HEADS, 2, TOK, DH)),
         shape((HEADS, 2, TOK, DH), BF16), shape((HEADS, 2, DH, TOK), BF16),
         shape((1,), jnp.int32)],
        flops=1 << 30,
        after=1,
        scratch=[pltpu.VMEM((BLOCK, 3 * BLOCK), BF16), pltpu.VMEM((HEADS, TOK), F32)],
    )(packed, core, *seqs, ld, *maps)
    scanned = small(
        scan_body, "scan", 1, pltpu.VMEM((CHIPS * ROWS, DH), F32),
        pl.BlockSpec(memory_space=pltpu.VMEM), smem=1,
    )(mark, swapped.reshape(CHIPS * (ROWS + 1), DH))
    inc = exchange(scanned.reshape(CHIPS, ROWS * DH), ("z", "x")).reshape(HEADS, DH, DH)
    passed = small(
        pass_body, "pass", 2, pltpu.VMEM((HEADS, DH, DH), F32),
        pl.BlockSpec(memory_space=pltpu.VMEM),
    )(mine, inc)
    recv = swap_cores(passed)
    gp_dims = (HEADS, 2, TOK, DH)
    st_dims = (HEADS, 4, DH, DH)
    half = pltpu.VMEM((HEADS, DH, DH), F32)
    gp, st, mine, send = streamed(
        k3a_body, "k3a",
        [pltpu.VMEM((HEADS, 2, DH, TOK), BF16), pltpu.VMEM((HEADS, 4, TOK, DH), BF16)],
        [pltpu.VMEM(gp_dims, BF16), pltpu.VMEM(st_dims, BF16)], [False, False, True, True],
        [pltpu.HBM(gp_dims, BF16), pltpu.HBM(st_dims, BF16), half, half],
        whole_ins=[pl.BlockSpec(memory_space=pltpu.VMEM)] * 5, grant=20 << 20,
    )(core, inc, recv, own, v, g,
      *(pltpu.with_memory_space_constraint(x, pltpu.HBM) for x in (tr, ab)))
    recv = swap_cores(send)
    chip = small(add_body, "add", 2, MAT, whole(HEADS, DH, DH))(mine, recv)
    pieces = exchange(chip.reshape(16, -1), ("x", "dp"))
    rows = HEADS * DH // 16
    wide = [per_head(2, TOK, DH, heads=WIDE)]
    out, gv, mark = call(
        k3b_body, "k3b",
        [smem()] + wide * 2 + [per_head(4, DH, DH, heads=WIDE)],
        [seq(WIDE)] * 2 + [smem()],
        [SEQ_B] * 2 + [shape((1,), jnp.int32)],
        flops=1 << 30,
        after=1,
        grid=HEADS // WIDE,
    )(chip, core, ov, dec, st)
    spread = small(
        spread_first_body, "spread_z", 1, pltpu.HBM((8, rows, DH), F32), whole(8, rows, DH), smem=1
    )(mark, pieces.reshape(16, rows, DH))
    pieces = exchange(spread.reshape(8, -1), "z")
    gq, gk, mark = call(
        k3c_body, "k3c",
        [smem()] + wide + [per_head(DH, DH, heads=WIDE)] * 2,
        [seq(WIDE)] * 2 + [smem()],
        [SEQ_B] * 2 + [shape((1,), jnp.int32)],
        flops=1 << 30,
        after=1,
        grid=HEADS // WIDE,
    )(spread, core, gp, *maps)
    spread = small(
        spread_first_body, "spread_xy", 1, shape((16, rows, DH)), whole(16, rows, DH), smem=1
    )(mark, pieces.reshape(8, rows, DH))
    own = exchange(spread.reshape(16, -1), ("x", "dp")).reshape(HEADS, DH, DH)
    other = swap_cores(own)
    first = core[0] == 0
    query_map_grad = jnp.where(first, own, other)
    key_map_grad = jnp.where(first, other, own)
    return (out[None], gq[None], gk[None], gv[None], query_map_grad, key_map_grad)


def solution(mesh):
    fine = Mesh(mesh.devices.reshape(8, 4, 2, 4), ("z", "x", "c", "dp"))
    ctx = ("z", "x", "c")
    act = P("dp", ctx, None)
    return jax.shard_map(
        local,
        mesh=fine,
        in_specs=(act, act, act, P("dp", None, ctx), act, P(), P()),
        out_specs=(act, act, act, act, P(), P()),
        check_vma=False,
    )
```

```python
import math

import jax
import jax.numpy as jnp
from jax import lax
from jax.experimental import pallas as pl
from jax.experimental.pallas import tpu as pltpu
from jax.sharding import Mesh, PartitionSpec as P

BLOCK = 256
HEADS = 8
DH = 128
TOK = 512
HPB = 2
WIDE = 4
SCALE = 1.0 / (DH * math.sqrt(BLOCK))
F32 = jnp.float32
BF16 = jnp.bfloat16
CHIPS = 32
ROWS = HEADS * DH // CHIPS


def dot(a, b, dims=((1,), (0,))):
    return lax.dot_general(a, b, (dims, ((), ())), preferred_element_type=F32)


NT = ((1,), (1,))
TN = ((0,), (0,))


def split3(x):
    hi = x.astype(BF16)
    rest = x - hi.astype(F32)
    mid = rest.astype(BF16)
    low = (rest - mid.astype(F32)).astype(BF16)
    return jnp.concatenate([hi, mid, low], axis=1)


def lower3():
    t = lax.broadcasted_iota(jnp.int32, (BLOCK, BLOCK), 0)
    s = lax.broadcasted_iota(jnp.int32, (BLOCK, BLOCK), 1)
    low = jnp.where(s <= t, 1.0, 0.0).astype(BF16)
    return jnp.concatenate([low, low, low], axis=1)


def cumul_cols(low, row):
    return dot(low, split3(jnp.broadcast_to(row, (DH, BLOCK))), NT)


def cumul_rows(low, rows):
    return dot(split3(rows), low, NT)


def sigmoid(u):
    return jax.nn.sigmoid(u)


def columns(ref, h):
    return ref.at[:, pl.ds(pl.multiple_of(h * DH, DH), DH)]


def head_copies(srcs, bufs, sems, h):
    return [
        pltpu.make_async_copy(columns(src, h) if len(src.shape) == 2 else src.at[h],
                              buf.at[h], sems.at[j, h])
        for j, (src, buf) in enumerate(zip(srcs, bufs))
    ]


def over_heads(srcs, bufs, sems, outs, out_sems, work, together=1):
    for h in range(HEADS):
        for copy in head_copies(srcs, bufs, sems, h):
            copy.start()

    def back(h):
        return [
            pltpu.make_async_copy(buf.at[h], dst.at[h], out_sems.at[j, h])
            for j, (buf, dst) in enumerate(outs)
        ]

    def some(step, carry):
        for i in range(HPB):
            for copy in head_copies(srcs, bufs, sems, step * HPB + i):
                copy.wait()
        for i in range(0, HPB, together):
            work(step * HPB + i)
        for i in range(HPB):
            for copy in back(step * HPB + i):
                copy.start()
        return carry

    lax.fori_loop(0, HEADS // HPB, some, 0)
    for h in range(HEADS):
        for copy in back(h):
            copy.wait()


def k1_body(core, ld_ref, q, k, v, g, wq, wk, mine_ref, send_ref, own,
            q_ref, k_ref, v_ref, g_ref, wq_ref, wk_ref, own_ref, cum_ref, sems, out_sems):
    first = core[0] == 0
    low = lower3()
    for b in range(2):
        rows = slice(b * BLOCK, (b + 1) * BLOCK)
        cum_ref[:, rows] = cumul_rows(low, ld_ref[:, rows])

    def both(ref, w_ref, h):
        zero = jnp.zeros((DH, DH), BF16)
        maps = jnp.concatenate([
            jnp.concatenate([w_ref[h], zero], axis=1),
            jnp.concatenate([zero, w_ref[h + 1]], axis=1),
        ], axis=0)
        return dot(maps, jnp.concatenate([ref[h], ref[h + 1]], axis=1), ((0,), (1,)))

    def pair(h):
        two_q, two_k = both(q_ref, wq_ref, h), both(k_ref, wk_ref, h)
        for i in range(2):
            work(h + i, two_q[i * DH:(i + 1) * DH], two_k[i * DH:(i + 1) * DH])

    def work(h, all_q, all_k):
        ups, cons, tots = [], [], []
        for b in range(2):
            rows = slice(b * BLOCK, (b + 1) * BLOCK)
            cum = cum_ref[pl.ds(h, 1), rows]
            tot = cum[:, BLOCK - 1:BLOCK]
            pre_q = all_q[:, rows]
            pre_k = all_k[:, rows]
            qf = (pre_q * sigmoid(pre_q)).astype(BF16)
            kf = (pre_k * sigmoid(pre_k)).astype(BF16)
            qdec = (qf.astype(F32) * jnp.exp(cum)).astype(BF16)
            kdec = (kf.astype(F32) * jnp.exp(tot - cum)).astype(BF16)
            ups.append(dot(kdec, v_ref[h, rows]))
            cons.append(dot(qdec, g_ref[h, rows]))
            tots.append(jnp.broadcast_to(tot, (8, DH)))
        d0, d1 = jnp.exp(tots[0]), jnp.exp(tots[1])
        up = d1[0:1] * ups[0] + ups[1]
        con = cons[0] + d0[0:1] * cons[1]
        mine_ref[h, 0:DH, :] = jnp.where(first, up, con)
        send_ref[h, 0:DH, :] = jnp.where(first, con, up)
        mine_ref[h, DH:DH + 8, :] = d0 * d1
        send_ref[h, DH:DH + 8, :] = d0 * d1
        own_ref[h, 0:DH, :] = ups[0]
        own_ref[h, DH:2 * DH, :] = cons[1]
        own_ref[h, 2 * DH:2 * DH + 8, :] = d0
        own_ref[h, 2 * DH + 8:, :] = d1

    over_heads((q, k, v, g, wq, wk), (q_ref, k_ref, v_ref, g_ref, wq_ref, wk_ref), sems,
               [(own_ref, own)], out_sems, pair, together=2)


def combine_body(mine_ref, recv_ref, out_ref):
    for h in range(HEADS):
        other = recv_ref[h, DH:DH + 1, :]
        agg = other * mine_ref[h, 0:DH, :] + recv_ref[h, 0:DH, :]
        both = other * mine_ref[h, DH:DH + 1, :]
        for part in range(DH // ROWS):
            at = (h * (DH // ROWS) + part) * (ROWS + 1)
            out_ref[at:at + ROWS, :] = agg[part * ROWS:(part + 1) * ROWS, :]
            out_ref[at + ROWS:at + ROWS + 1, :] = both


def scan_body(core, in_ref, out_ref):
    first = core[0] == 0

    def pieces(k):
        at = k * (ROWS + 1)
        return in_ref[at:at + ROWS, :], in_ref[at + ROWS:at + ROWS + 1, :]

    state = jnp.zeros((ROWS, DH), F32)
    for k in range(CHIPS):
        out_ref[k * ROWS:(k + 1) * ROWS, :] = state
        part, decay = pieces(k)
        state = decay * state + part
    state = jnp.zeros((ROWS, DH), F32)
    for k in range(CHIPS - 1, -1, -1):
        rows = slice(k * ROWS, (k + 1) * ROWS)
        out_ref[rows, :] = jnp.where(first, out_ref[rows, :], state)
        part, decay = pieces(k)
        state = decay * state + part


def k2_body(core, q_ref, k_ref, v_ref, g_ref, ld_ref, wq_ref, wk_ref,
            ab_ref, ov_ref, dec_ref, tr_ref, mark_ref, low_ref, cum_ref):
    step = pl.program_id(0)

    @pl.when(step == 0)
    def _():
        low_ref[...] = lower3()
        for b in range(2):
            rows = slice(b * BLOCK, (b + 1) * BLOCK)
            cum_ref[:, rows] = cumul_rows(low_ref[...], ld_ref[:, rows])

    t = lax.broadcasted_iota(jnp.int32, (BLOCK, BLOCK), 0)
    s = lax.broadcasted_iota(jnp.int32, (BLOCK, BLOCK), 1)
    causal = s <= t
    for i in range(HPB):
        lanes = slice(i * DH, (i + 1) * DH)
        tr_ref[i, 0] = q_ref[:, lanes].T
        tr_ref[i, 1] = k_ref[:, lanes].T
        for b in range(2):
            rows = slice(b * BLOCK, (b + 1) * BLOCK)
            head = pl.ds(step * HPB + i, 1)
            cum = cumul_cols(low_ref[...], ld_ref[head, rows])
            across = cum_ref[head, rows]
            tot = cum[BLOCK - 1:BLOCK, :]
            wide = jnp.concatenate([cum, cum], axis=1)
            weights = jnp.exp(jnp.where(causal, wide - across, -1e9))
            v, g = v_ref[rows, lanes], g_ref[rows, lanes]
            pre_q = dot(q_ref[rows, lanes], wq_ref[i])
            pre_k = dot(k_ref[rows, lanes], wk_ref[i])
            sig_q, sig_k = sigmoid(pre_q), sigmoid(pre_k)
            qf, kf = (pre_q * sig_q).astype(BF16), (pre_k * sig_k).astype(BF16)
            probs = (dot(qf, kf, NT) * weights).astype(BF16)
            grads = (dot(g, v, NT) * weights).astype(BF16)
            ov_ref[i, 0, rows] = SCALE * dot(probs, v)
            ov_ref[i, 1, rows] = SCALE * dot(probs, g, TN)
            early, late = jnp.exp(cum), jnp.exp(tot - cum)
            dec_ref[i, 0, rows] = (qf.astype(F32) * early).astype(BF16)
            dec_ref[i, 1, rows] = (kf.astype(F32) * late).astype(BF16)
            slope_q = SCALE * (sig_q * (1.0 + pre_q * (1.0 - sig_q)))
            ab_ref[i, 0, rows] = (dot(grads, kf) * slope_q).astype(BF16)
            ab_ref[i, 1, rows] = (early * slope_q).astype(BF16)
            slope_k = SCALE * (sig_k * (1.0 + pre_k * (1.0 - sig_k)))
            ab_ref[i, 2, rows] = (dot(grads, qf, TN) * slope_k).astype(BF16)
            ab_ref[i, 3, rows] = (late * slope_k).astype(BF16)
    mark_ref[0] = core[0]


def k3a_body(core, inc_ref, recv_ref, own_ref, v_ref, g_ref, tr, ab,
             gp, st, mine_ref, send_ref, tr_ref, ab_ref, gp_ref, st_ref, sems, out_sems):
    first = core[0] == 0

    def diagonal(a, b):
        zero = jnp.zeros((DH, DH), BF16)
        return jnp.concatenate([
            jnp.concatenate([a, zero], axis=1), jnp.concatenate([zero, b], axis=1)
        ], axis=0)

    def rounded(h):
        inc, recv = inc_ref[h], recv_ref[h]
        state = jnp.where(first, inc, recv)
        after = jnp.where(first, recv, inc)
        d0, d1 = own_ref[h, 2 * DH:2 * DH + 1, :], own_ref[h, 2 * DH + 8:2 * DH + 9, :]
        four = (
            state.astype(BF16),
            (d0 * state + own_ref[h, 0:DH, :]).astype(BF16),
            (own_ref[h, DH:2 * DH, :] + d1 * after).astype(BF16),
            after.astype(BF16),
        )
        for j in range(4):
            st_ref[h, j] = four[j]
        return four

    def pair(h):
        lanes = pl.ds(pl.multiple_of(h * DH, 2 * DH), 2 * DH)
        one, two = rounded(h), rounded(h + 1)
        for b in range(2):
            rows = slice(b * BLOCK, (b + 1) * BLOCK)
            from_state = dot(g_ref[rows, lanes], diagonal(one[b], two[b]), NT)
            from_after = dot(v_ref[rows, lanes], diagonal(one[2 + b], two[2 + b]), NT)
            for i in range(2):
                cols = slice(i * DH, (i + 1) * DH)
                for j, x in enumerate((from_state, from_after)):
                    gp_ref[h + i, j, rows] = (
                        ab_ref[h + i, 2 * j, rows].astype(F32)
                        + ab_ref[h + i, 2 * j + 1, rows].astype(F32) * x[:, cols]
                    ).astype(BF16)
        for i in range(2):
            part_q = dot(tr_ref[h + i, 0], gp_ref[h + i, 0])
            part_k = dot(tr_ref[h + i, 1], gp_ref[h + i, 1])
            mine_ref[h + i] = jnp.where(first, part_q, part_k)
            send_ref[h + i] = jnp.where(first, part_k, part_q)

    over_heads((tr, ab), (tr_ref, ab_ref), sems,
               [(gp_ref, gp), (st_ref, st)], out_sems, pair, together=2)


def k3b_body(core, ov_ref, dec_ref, st_ref, gp_ref, wq_ref, wk_ref,
             out_ref, gq_ref, gk_ref, gv_ref, mark_ref):
    mark_ref[0] = core[0]
    for i in range(WIDE):
        lanes = slice(i * DH, (i + 1) * DH)
        for b in range(2):
            rows = slice(b * BLOCK, (b + 1) * BLOCK)
            out_ref[rows, lanes] = (
                ov_ref[i, 0, rows] + SCALE * dot(dec_ref[i, 0, rows], st_ref[i, b])
            ).astype(BF16)
            gv_ref[rows, lanes] = (
                ov_ref[i, 1, rows] + SCALE * dot(dec_ref[i, 1, rows], st_ref[i, 2 + b])
            ).astype(BF16)
            gq_ref[rows, lanes] = dot(gp_ref[i, 0, rows], wq_ref[i], NT).astype(BF16)
            gk_ref[rows, lanes] = dot(gp_ref[i, 1, rows], wk_ref[i], NT).astype(BF16)


def add_body(a_ref, b_ref, out_ref):
    out_ref[...] = a_ref[...] + b_ref[...]


def pass_body(mine_ref, inc_ref, out_ref):
    for h in range(HEADS):
        out_ref[h] = mine_ref[h, DH:DH + 1, :] * inc_ref[h] + mine_ref[h, 0:DH, :]


def spread_first_body(core, in_ref, out_ref):
    spread_body(in_ref, out_ref)


def spread_body(in_ref, out_ref):
    total = in_ref[0]
    for k in range(1, in_ref.shape[0]):
        total = total + in_ref[k]
    for k in range(out_ref.shape[0]):
        out_ref[k] = total


def smem():
    return pl.BlockSpec(memory_space=pltpu.SMEM)


def seq(heads=HPB):
    return pl.BlockSpec((TOK, heads * DH), lambda i: (0, i))


def per_head(*tail, heads=HPB):
    zeros = (0,) * len(tail)
    return pl.BlockSpec((heads,) + tail, lambda i: (i,) + zeros)


def whole(*shape):
    zeros = (0,) * len(shape)
    return pl.BlockSpec(shape, lambda i: zeros)


def shape(dims, kind=F32):
    return jax.ShapeDtypeStruct(dims, kind)


def call(body, name, ins, outs, out_shapes, flops=0, grid=HEADS // HPB, after=0,
         scratch=(), grant=None):
    return pl.pallas_call(
        lambda *refs: body(*refs[after:]),
        grid=(grid,),
        in_specs=[pl.BlockSpec(memory_space=pltpu.HBM)] * after + ins,
        out_specs=outs,
        out_shape=out_shapes,
        scratch_shapes=scratch,
        name=name,
        cost_estimate=pl.CostEstimate(flops=flops, transcendentals=0, bytes_accessed=1 << 20),
        compiler_params=pltpu.CompilerParams(
            dimension_semantics=("arbitrary",), vmem_limit_bytes=grant
        ),
    )


def streamed(body, name, slots, back, held, out_shapes, whole_ins=(), scratch=(),
             grant=None):
    raw = pl.BlockSpec(memory_space=pltpu.HBM)
    kept = pl.BlockSpec(memory_space=pltpu.VMEM)
    return pl.pallas_call(
        body,
        grid=(1,),
        in_specs=[smem()] + list(whole_ins) + [raw] * len(slots),
        out_specs=[kept if here else raw for here in held],
        out_shape=out_shapes,
        scratch_shapes=list(slots) + list(back) + list(scratch) + [
            pltpu.SemaphoreType.DMA((len(slots), HEADS)),
            pltpu.SemaphoreType.DMA((len(back), HEADS)),
        ],
        name=name,
        compiler_params=pltpu.CompilerParams(
            dimension_semantics=("arbitrary",), vmem_limit_bytes=grant
        ),
    )


def small(body, name, ins, out_shape, out_spec, smem=0, after=0):
    vmem = pl.BlockSpec(memory_space=pltpu.VMEM)
    return pl.pallas_call(
        lambda *refs: body(*refs[after:]),
        grid=(1,),
        in_specs=[pl.BlockSpec(memory_space=pltpu.HBM)] * after
        + [pl.BlockSpec(memory_space=pltpu.SMEM)] * smem + [vmem] * ins,
        out_specs=out_spec,
        out_shape=out_shape,
        name=name,
        compiler_params=pltpu.CompilerParams(vmem_limit_bytes=8 << 20),
    )


def exchange(x, axes):
    return lax.all_to_all(x, axes, 0, 0, tiled=True)


def swap_cores(x):
    return lax.ppermute(x, "c", [(0, 1), (1, 0)])


SEQ_B = shape((TOK, HEADS * DH), BF16)
SEQ_F = shape((TOK, HEADS * DH), F32)
MAT = shape((HEADS, DH, DH), F32)


def local(query, key, value, log_decay, grad_out, query_map, key_map):
    core = lax.axis_index("c").astype(jnp.int32).reshape(1)
    q, k, v, g = (a[0] for a in (query, key, value, grad_out))
    ld = log_decay[0]
    maps = (query_map, key_map)
    seqs = (q, k, v, g)
    ld_spec = whole(HEADS, TOK)
    map_specs = [per_head(DH, DH)] * 2
    slot = pltpu.VMEM((HEADS, TOK, DH), BF16)
    square = pltpu.VMEM((HEADS, DH, DH), BF16)
    cut = pltpu.VMEM((HEADS, DH + 8, DH), F32)
    own_dims = (HEADS, 2 * DH + 16, DH)
    mine, send, own = streamed(
        k1_body, "k1", [slot] * 4 + [square] * 2, [pltpu.VMEM(own_dims, F32)],
        [True, True, False], [cut, cut, pltpu.HBM(own_dims, F32)],
        whole_ins=[ld_spec], scratch=[pltpu.VMEM((HEADS, TOK), F32)],
    )(core, ld, *seqs, *maps)
    recv = swap_cores(send)
    packed = small(
        combine_body, "combine", 2, shape((CHIPS * (ROWS + 1), DH)), whole(CHIPS * (ROWS + 1), DH),
    )(mine, recv)
    swapped = exchange(packed.reshape(CHIPS, (ROWS + 1) * DH), ("z", "x"))
    ab, ov, dec, tr, mark = call(
        k2_body, "k2",
        [smem()] + [seq()] * 4 + [ld_spec] + map_specs,
        [per_head(4, TOK, DH), per_head(2, TOK, DH), per_head(2, TOK, DH), per_head(2, DH, TOK),
         smem()],
        [shape((HEADS, 4, TOK, DH), BF16), shape((HEADS, 2, TOK, DH)),
         shape((HEADS, 2, TOK, DH), BF16), shape((HEADS, 2, DH, TOK), BF16),
         shape((1,), jnp.int32)],
        flops=1 << 30,
        after=1,
        scratch=[pltpu.VMEM((BLOCK, 3 * BLOCK), BF16), pltpu.VMEM((HEADS, TOK), F32)],
    )(packed, core, *seqs, ld, *maps)
    scanned = small(
        scan_body, "scan", 1, pltpu.VMEM((CHIPS * ROWS, DH), F32),
        pl.BlockSpec(memory_space=pltpu.VMEM), smem=1,
    )(mark, swapped.reshape(CHIPS * (ROWS + 1), DH))
    inc = exchange(scanned.reshape(CHIPS, ROWS * DH), ("z", "x")).reshape(HEADS, DH, DH)
    passed = small(
        pass_body, "pass", 2, pltpu.VMEM((HEADS, DH, DH), F32),
        pl.BlockSpec(memory_space=pltpu.VMEM),
    )(mine, inc)
    recv = swap_cores(passed)
    gp_dims = (HEADS, 2, TOK, DH)
    st_dims = (HEADS, 4, DH, DH)
    half = pltpu.VMEM((HEADS, DH, DH), F32)
    gp, st, mine, send = streamed(
        k3a_body, "k3a",
        [pltpu.VMEM((HEADS, 2, DH, TOK), BF16), pltpu.VMEM((HEADS, 4, TOK, DH), BF16)],
        [pltpu.VMEM(gp_dims, BF16), pltpu.VMEM(st_dims, BF16)], [False, False, True, True],
        [pltpu.HBM(gp_dims, BF16), pltpu.HBM(st_dims, BF16), half, half],
        whole_ins=[pl.BlockSpec(memory_space=pltpu.VMEM)] * 5, grant=20 << 20,
    )(core, inc, recv, own, v, g,
      *(pltpu.with_memory_space_constraint(x, pltpu.HBM) for x in (tr, ab)))
    recv = swap_cores(send)
    chip = small(add_body, "add", 2, MAT, whole(HEADS, DH, DH))(mine, recv)
    pieces = exchange(chip.reshape(16, -1), ("x", "dp"))
    rows = HEADS * DH // 16
    out, gq, gk, gv, mark = call(
        k3b_body, "k3b",
        [smem(), per_head(2, TOK, DH, heads=WIDE), per_head(2, TOK, DH, heads=WIDE),
         per_head(4, DH, DH, heads=WIDE), per_head(2, TOK, DH, heads=WIDE)]
        + [per_head(DH, DH, heads=WIDE)] * 2,
        [seq(WIDE)] * 4 + [smem()],

        [SEQ_B] * 4 + [shape((1,), jnp.int32)],
        flops=1 << 30,
        after=1,
        grid=HEADS // WIDE,
    )(chip, core, ov, dec, st, gp, *maps)
    spread = small(spread_first_body, "spread_z", 1, shape((8, rows, DH)), whole(8, rows, DH), smem=1)(
        mark, pieces.reshape(16, rows, DH)
    )
    pieces = exchange(spread.reshape(8, -1), "z")
    spread = small(spread_body, "spread_xy", 1, shape((16, rows, DH)), whole(16, rows, DH))(
        pieces.reshape(8, rows, DH)
    )
    own = exchange(spread.reshape(16, -1), ("x", "dp")).reshape(HEADS, DH, DH)
    other = swap_cores(own)
    first = core[0] == 0
    query_map_grad = jnp.where(first, own, other)
    key_map_grad = jnp.where(first, other, own)
    return (out[None], gq[None], gk[None], gv[None], query_map_grad, key_map_grad)


def solution(mesh):
    fine = Mesh(mesh.devices.reshape(8, 4, 2, 4), ("z", "x", "c", "dp"))
    ctx = ("z", "x", "c")
    act = P("dp", ctx, None)
    return jax.shard_map(
        local,
        mesh=fine,
        in_specs=(act, act, act, P("dp", None, ctx), act, P(), P()),
        out_specs=(act, act, act, act, P(), P()),
        check_vma=False,
    )
```
